512 devices in a mesh: seq: 128 (over z, x, core), dp: 4 (over y).
Axes of the slice: x: 4, y: 4, z: 16, core: 2. Of those that a mesh axis runs over, the one named last changes fastest.
Arguments:
- queries: bfloat16 [8192, 512], P(('dp', 'seq')), parts along dimension 0, may hold values from -6 to 6
- keys: bfloat16 [8192, 512], P(('dp', 'seq')), parts along dimension 0, may hold values from -6 to 6
- values: bfloat16 [8192, 512], P(('dp', 'seq')), parts along dimension 0, may hold values from -6 to 6
- residual: bfloat16 [8192, 1024], P(('dp', 'seq')), parts along dimension 0, may hold values from -16 to 16
- lengths: int32 [4], P('dp'), parts along dimension 0, may hold values from 1024 to 2048
- out_proj: bfloat16 [512, 1024], replicated, may hold values from -0.75 to 0.75
- ln_gain: float32 [1024], replicated, may hold values from 0.1 to 1.9
- ln_bias: float32 [1024], replicated, may hold values from -3 to 3
- conv_in: bfloat16 [1024, 1024], replicated, may hold values from -0.1875 to 0.1875
- taps: float32 [31, 512], replicated, may hold values from -1 to 1
- bn_scale: float32 [512], replicated, may hold values from 0.5 to 2
- bn_shift: float32 [512], replicated, may hold values from -3 to 3
- conv_out: bfloat16 [512, 1024], replicated, may hold values from -0.25 to 0.25
Outputs:
- block_out: bfloat16 [8192, 1024], P(('dp', 'seq')), parts along dimension 0
The draws below stay inside these ranges and needn't reach their ends.
There are 4 independent parts, one for each index of `dp`. The reference program is written for one: setup_inputs(seed, part) draws one part's arguments, and reference() takes and returns one part's arrays. A program takes and returns all parts, laid end to end along the dimension named above; an argument that names none is the same for every part. Nothing has to cross between parts.
All inputs are finite; a program needn't handle non-finite values.
Results may differ from the reference program's by a relative error of at most 0.0075.
Values may be sent and summed in bfloat16 or wider, within the bound.
A program may use at most 64 MiB of HBM per device.

```python
import math
import jax
import jax.numpy as jnp
from jax import lax

D = 1024
HEADS = 8
HEAD_DIM = 64
CONV_CH = 512
KERNEL = 31
TOK_DEV = 16
ATT = 512
FRAMES = 2048
N_SEQ = 128


def attention_pairs(key):
    width = HEADS * HEAD_DIM
    base_query = jnp.clip(1.6 * jax.random.normal(jax.random.fold_in(key, 11), (FRAMES, width), jnp.float32), -6.0, 6.0)
    base_key = jnp.clip(1.6 * jax.random.normal(jax.random.fold_in(key, 12), (FRAMES, width), jnp.float32), -6.0, 6.0)
    return (base_query, base_key)


def draw_queries(key, part):
    return attention_pairs(key)[0].astype(jnp.bfloat16)


def draw_keys(key, part):
    return attention_pairs(key)[1].astype(jnp.bfloat16)


def draw_residual(key, part):
    column_scale = jnp.exp(jax.random.uniform(jax.random.fold_in(key, 21), (1, D), jnp.float32, math.log(0.3), math.log(3.0)))
    base = jax.random.normal(jax.random.fold_in(key, 22), (FRAMES, D), jnp.float32)
    return jnp.clip(base * column_scale, -16.0, 16.0).astype(jnp.bfloat16)


def shard_levels(own_key, shape, cuts, least, largest):
    def one(dim, blocks):
        heights = jax.random.uniform(jax.random.fold_in(jax.random.fold_in(own_key, 6), dim), (blocks,), jnp.float32, least / len(cuts), largest / len(cuts))
        return jnp.repeat(jnp.exp(heights), shape[dim] // blocks).reshape((-1,) + (1,) * (len(shape) - dim - 1))

    gain = one(*cuts[0])
    for cut in cuts[1:]:
        gain = gain * one(*cut)
    return gain


def bell_draw(stream_key, shape, scale, limit, split=(), kind=jnp.bfloat16):
    result = scale * jax.random.normal(stream_key, shape, jnp.float32)
    if split:
        result = result * shard_levels(stream_key, shape, split, -0.22, 0.18)
    return jnp.clip(result, -limit, limit).astype(kind)


def setup_inputs(seed: int = 0, part: int = 0) -> dict:
    key_list = jax.random.split(jax.random.key(seed), 14)
    own_keys = jax.random.split(jax.random.fold_in(key_list[13], part), 14)
    queries = draw_queries(jax.random.fold_in(jax.random.fold_in(key_list[13], part), 71), part)
    keys = draw_keys(jax.random.fold_in(jax.random.fold_in(key_list[13], part), 71), part)
    values = bell_draw(own_keys[2], (FRAMES, ATT), 1.0, 6.0, ((0, 128),))
    residual = draw_residual(jax.random.fold_in(jax.random.fold_in(key_list[13], part), 71), part)
    lengths = jax.random.randint(own_keys[4], (1,), FRAMES // 2, FRAMES + 1).astype(jnp.int32)
    out_proj = bell_draw(key_list[5], (ATT, D), HEAD_DIM ** -0.5, 0.75)
    ln_gain = jnp.clip(1.0 + 0.18 * jax.random.normal(key_list[6], (D,), jnp.float32), 0.1, 1.9)
    ln_bias = bell_draw(key_list[7], (D,), 0.5, 3.0, (), jnp.float32)
    conv_in = bell_draw(key_list[8], (D, 2 * CONV_CH), D ** -0.5, 0.1875)
    taps = bell_draw(key_list[9], (KERNEL, CONV_CH), KERNEL ** -0.5, 1.0, (), jnp.float32)
    bn_scale = jnp.clip(jnp.exp(jax.random.uniform(key_list[10], (CONV_CH,), jnp.float32, math.log(0.5), math.log(2.0))), 0.5, 2.0)
    bn_shift = bell_draw(key_list[11], (CONV_CH,), 0.5, 3.0, (), jnp.float32)
    conv_out = bell_draw(key_list[12], (CONV_CH, D), CONV_CH ** -0.5, 0.25)
    return {"queries": queries, "keys": keys, "values": values, "residual": residual, "lengths": lengths, "out_proj": out_proj, "ln_gain": ln_gain, "ln_bias": ln_bias, "conv_in": conv_in, "taps": taps, "bn_scale": bn_scale, "bn_shift": bn_shift, "conv_out": conv_out}


def reference(queries, keys, values, residual, lengths, out_proj, ln_gain, ln_bias, conv_in, taps, bn_scale, bn_shift, conv_out):
    frame_ids = jnp.arange(FRAMES, dtype=jnp.int32)
    valid_mask = frame_ids < lengths[0].astype(jnp.int32)
    valid = valid_mask.astype(jnp.float32)
    query_heads = queries.reshape(FRAMES, HEADS, HEAD_DIM)
    key_heads = keys.reshape(FRAMES, HEADS, HEAD_DIM).astype(jnp.float32)
    value_heads = values.reshape(FRAMES, HEADS, HEAD_DIM).astype(jnp.float32)
    factor = 1.0 / math.sqrt(HEAD_DIM)

    def attend_rows(number):
        start = (number * TOK_DEV).astype(jnp.int32)
        query_block = lax.dynamic_slice_in_dim(query_heads, start, TOK_DEV, 0).astype(jnp.float32)
        scores = jnp.einsum('qhd,khd->hqk', query_block, key_heads) * factor
        scores = jnp.where(valid_mask[None, None, :], scores, -1e+30)
        highest = lax.optimization_barrier(jnp.max(scores, axis=-1))
        powered = jnp.exp(scores - highest[:, :, None])
        totals = lax.optimization_barrier(jnp.sum(powered, axis=-1))
        weights = lax.optimization_barrier(powered.astype(jnp.bfloat16)).astype(jnp.float32)
        summed = jnp.einsum('hqk,khd->qhd', weights, value_heads)
        context_rows = summed / jnp.transpose(totals)[:, :, None]
        return context_rows.astype(jnp.bfloat16).reshape(TOK_DEV, HEADS * HEAD_DIM)
    context = lax.map(attend_rows, jnp.arange(N_SEQ, dtype=jnp.int32)).reshape(FRAMES, HEADS * HEAD_DIM)
    mixed = residual.astype(jnp.float32) + valid[:, None] * jnp.dot(context, out_proj, preferred_element_type=jnp.float32)
    average = lax.optimization_barrier(jnp.mean(mixed, axis=-1, keepdims=True))
    centred = mixed - average
    variance = lax.optimization_barrier(jnp.mean(centred * centred, axis=-1, keepdims=True))
    normed = (centred * lax.rsqrt(variance + 1e-05) * ln_gain + ln_bias).astype(jnp.bfloat16)
    lifted = jnp.dot(normed, conv_in, preferred_element_type=jnp.float32)
    gated = (valid[:, None] * lifted[:, :CONV_CH] * jax.nn.sigmoid(lifted[:, CONV_CH:])).astype(jnp.bfloat16)
    margin = KERNEL // 2
    widened = jnp.pad(lax.optimization_barrier(gated).astype(jnp.float32), ((margin, margin), (0, 0)))
    filtered = taps[0] * widened[0:FRAMES]
    for offset in range(1, KERNEL):
        filtered = filtered + taps[offset] * widened[offset:offset + FRAMES]
    shifted = filtered * bn_scale + bn_shift
    activated = (shifted * jax.nn.sigmoid(shifted)).astype(jnp.bfloat16)
    return (mixed + jnp.dot(activated, conv_out, preferred_element_type=jnp.float32)).astype(jnp.bfloat16)
```

```python
import functools
import math

import jax
import jax.numpy as jnp
from jax import lax
from jax.experimental import pallas as pl
from jax.experimental.pallas import tpu as pltpu
from jax.sharding import PartitionSpec as P

MESH = pl.DeviceIdType.MESH
BF16 = jnp.bfloat16
F32 = jnp.float32

NZ = 16
SLAB = 8
ROWS = 16
HALF = 256
HEAD = 64


def slot_of(offset):
    return 2 * abs(offset) - (1 if offset > 0 else 0)


FIRST = (4, -4, 3, -3)
NEAR = (2, -2, 1, -1)
RELAYS = ((-4, 4), (-3, 4), (3, -4), (-4, 2), (4, -2), (-3, 2), (3, -2))


def landed(offset):
    return 15 if offset in (8, -8) else slot_of(offset)


def kernel(
    q_hbm, k_hbm, v_hbm, res_hbm, len_ref, wo_hbm, gain_hbm, bias_hbm, wi_hbm, taps_hbm, scale_hbm, shift_hbm, wc_hbm,
    out_ref,
    q_in, k_in, v_in, res, wo, gain, bias, wi, taps, scale, shift, wc,
    kv_own, kv, q_own, q_all, a_send, a_recv, ctx_own, ctx, gated,
    in_sem, kv_ss, kv_rs, q_ss, q_rs, r_ss, r_rs, a_ss, a_rs, c_ss, c_rs,
):
    me = lax.axis_index("seq")
    z = me // SLAB
    xc = lax.rem(me, SLAB)
    par = lax.rem(z, 2)
    other = 1 - par
    limit = len_ref[0]

    def at_z(offset):
        return lax.rem(z + offset + NZ, NZ) * SLAB + xc

    def at_slab(step):
        return z * SLAB + lax.rem(xc + step, SLAB)

    partner = (z + 1 - 2 * par) * SLAB + xc
    left = lax.rem(me + 127, 128)
    right = lax.rem(me + 1, 128)

    loads = [
        pltpu.make_async_copy(src, dst, in_sem.at[i])
        for i, (src, dst) in enumerate(
            (
                (k_hbm, k_in), (v_hbm, v_in), (q_hbm, q_in), (res_hbm, res.at[1]),
                (wo_hbm, wo), (wi_hbm, wi), (wc_hbm, wc),
                (gain_hbm, gain), (bias_hbm, bias), (taps_hbm, taps), (scale_hbm, scale), (shift_hbm, shift),
            )
        )
    ]
    for load in loads[:4]:
        load.start()

    barrier = pltpu.get_barrier_semaphore()
    greet = [at_z(d) for d in FIRST + NEAR] + [at_slab(i) for i in range(1, SLAB)] + [left, right]
    for target in greet:
        pl.semaphore_signal(barrier, inc=1, device_id={"seq": target}, device_id_type=MESH)
    for load in loads[4:]:
        load.start()
    for load in loads[:3]:
        load.wait()
    for g in range(2):
        kv_own[g, 0] = k_in[:, HALF * g : HALF * (g + 1)]
        kv_own[g, 1] = v_in[:, HALF * g : HALF * (g + 1)]
        q_own[g] = q_in[:, HALF * g : HALF * (g + 1)]
    kv[0] = kv_own[par]
    q_all[xc, par] = q_own[par]
    loads[3].wait()
    pl.semaphore_wait(barrier, len(greet))

    def remote(src, dst, ss, rs, target):
        return pltpu.make_async_remote_copy(
            src_ref=src, dst_ref=dst, send_sem=ss, recv_sem=rs, device_id={"seq": target}, device_id_type=MESH
        )

    def first(d):
        slot = slot_of(-d)
        g = lax.rem(par + abs(d), 2)
        return remote(kv_own.at[g], kv.at[slot], kv_ss.at[slot], kv_rs.at[slot], at_z(d))

    def relay(source, d):
        slot = landed(source - d)
        return remote(kv.at[slot_of(source)], kv.at[slot], kv_ss.at[slot], kv_rs.at[slot], at_z(d))

    def arrived(slot):
        remote(kv.at[slot], kv.at[slot], kv_ss.at[slot], kv_rs.at[slot], right).wait_recv()

    first_copies = [first(d) for d in FIRST + NEAR]
    q_first = remote(q_own.at[other], q_all.at[xc, par], q_ss.at[0], q_rs.at[0], partner)
    for copy in first_copies[:4]:
        copy.start()
    q_first.start()
    for copy in first_copies[4:]:
        copy.start()

    remote(q_own.at[other], q_all.at[xc, other], q_ss.at[0], q_rs.at[0], partner).wait_recv()
    q_copies = [
        remote(q_all.at[xc], q_all.at[xc], q_ss.at[i], q_rs.at[i], at_slab(i)) for i in range(1, SLAB)
    ]
    for copy in q_copies:
        copy.start()
    res_right = remote(res.at[1], res.at[0], r_ss.at[0], r_rs.at[0], right)
    res_left = remote(res.at[1], res.at[2], r_ss.at[1], r_rs.at[1], left)
    res_right.start()
    res_left.start()

    relay_copies = []
    seen = []
    for source, d in RELAYS:
        if source not in seen:
            arrived(slot_of(source))
            seen.append(source)
        copy = relay(source, d)
        copy.start()
        relay_copies.append(copy)

    for i in range(1, SLAB):
        sender = lax.rem(xc + SLAB - i, SLAB)
        remote(q_all.at[sender], q_all.at[sender], q_ss.at[i], q_rs.at[i], at_slab(i)).wait_recv()
    for offset in (1, -1, 2, -2):
        arrived(slot_of(offset))

    lane = lax.broadcasted_iota(jnp.int32, (1, 128), 1)
    low = lane < HEAD
    factor = 1.0 / math.sqrt(HEAD)

    queries = []
    for pair in range(2):
        tile = q_all[:, :, :, 128 * pair : 128 * (pair + 1)].reshape(256, 128) * jnp.asarray(factor, BF16)
        zero = jnp.zeros_like(tile)
        queries.append((jnp.where(low, tile, zero), jnp.where(low, zero, tile)))

    def chunk(part):
        slot = 8 * part + lane // ROWS
        away = (slot + 1) // 2
        offset = jnp.where(lax.rem(slot, 2) == 1, away, -away)
        source = lax.rem(z + offset + NZ, NZ)
        frame = (source * SLAB + xc) * ROWS + lax.rem(lane, ROWS)
        valid = frame < limit
        result = []
        for pair in range(2):
            cols = slice(128 * pair, 128 * (pair + 1))
            key = kv[8 * part : 8 * part + 8, 0, :, cols].reshape(128, 128)
            value = kv[8 * part : 8 * part + 8, 1, :, cols].reshape(128, 128)
            for half in range(2):
                scores = lax.dot_general(
                    queries[pair][half], key, (((1,), (1,)), ((), ())), preferred_element_type=F32
                )
                scores = jnp.where(valid, scores, -1e30)
                top = jnp.max(scores, axis=-1, keepdims=True)
                powered = jnp.exp(scores - top)
                total = jnp.sum(powered, axis=-1, keepdims=True)
                mixed_values = jnp.dot(powered.astype(BF16), value, preferred_element_type=F32)
                result.append((top, total, mixed_values))
        return result

    near = chunk(0)
    arrived(slot_of(-4)) if -4 not in seen else None
    for slot in range(9, 16):
        arrived(slot)
    far = chunk(1)

    stats = jnp.zeros((256, 128), F32)
    for pair in range(2):
        tiles = []
        for half in range(2):
            head = 2 * pair + half
            top_a, total_a, mixed_a = near[head]
            top_b, total_b, mixed_b = far[head]
            top = jnp.maximum(top_a, top_b)
            grow_a = jnp.exp(top_a - top)
            grow_b = jnp.exp(top_b - top)
            total = grow_a * total_a + grow_b * total_b
            inverse = 1.0 / total
            tiles.append((grow_a * inverse) * mixed_a + (grow_b * inverse) * mixed_b)
            level = top + jnp.log(total)
            for step in range(3):
                rounded = level.astype(BF16).astype(F32)
                stats = jnp.where(lane == 3 * head + step, rounded, stats)
                level = level - rounded
        a_send[:, 128 * pair : 128 * (pair + 1)] = jnp.where(low, tiles[0], tiles[1]).astype(BF16)
    a_send[:, HALF : HALF + 128] = stats.astype(BF16)

    a_copies = []
    for i in range(1, SLAB):
        owner = lax.rem(xc + i, SLAB)
        copy = remote(
            a_send.at[pl.ds(pl.multiple_of(owner * 32, 32), 32)], a_recv.at[xc], a_ss.at[i], a_rs.at[i], at_slab(i)
        )
        copy.start()
        a_copies.append(copy)
    a_recv[xc] = a_send[pl.ds(pl.multiple_of(xc * 32, 32), 32), :]
    row_id = lax.broadcasted_iota(jnp.int32, (128, HALF), 0)
    col_id = lax.broadcasted_iota(jnp.int32, (128, HALF), 1)
    spread = jnp.where(row_id // 3 == col_id // HEAD, 1.0, 0.0).astype(BF16)
    for i in range(1, SLAB):
        sender = lax.rem(xc + SLAB - i, SLAB)
        remote(a_recv.at[sender], a_recv.at[sender], a_ss.at[i], a_rs.at[i], at_slab(i)).wait_recv()
    parts = a_recv[:, :, :HALF].astype(F32)
    levels = jnp.dot(
        a_recv[:, :, HALF : HALF + 128].reshape(256, 128), spread, preferred_element_type=F32
    ).reshape(8, 32, HALF)
    weights = jnp.exp(levels - jnp.max(levels, axis=0, keepdims=True))
    context = jnp.sum(weights * parts, axis=0) / jnp.sum(weights, axis=0)
    ctx_own[...] = context.astype(BF16).reshape(2, ROWS, HALF)

    c_copies = []
    for where, (slab, start) in enumerate(((par, me), (other, partner))):
        for place, shift_by in ((0, 1), (2, 127), (1, 0)):
            if where == 0 and place == 1:
                continue
            target = lax.rem(start + shift_by, 128)
            copy = remote(
                ctx_own.at[slab], ctx.at[par, place], c_ss.at[where, place], c_rs.at[par, place], target
            )
            copy.start()
            c_copies.append(copy)
    ctx[par, 1] = ctx_own[par]

    for load in loads[4:]:
        load.wait()
    for place in (0, 2):
        for g in range(2):
            remote(ctx.at[g, place], ctx.at[g, place], c_ss.at[0, place], c_rs.at[g, place], right).wait_recv()
    remote(ctx.at[other, 1], ctx.at[other, 1], c_ss.at[1, 1], c_rs.at[other, 1], right).wait_recv()
    remote(res.at[1], res.at[0], r_ss.at[0], r_rs.at[0], right).wait_recv()
    remote(res.at[1], res.at[2], r_ss.at[1], r_rs.at[1], left).wait_recv()

    frames = (me - 1) * ROWS + lax.broadcasted_iota(jnp.int32, (48, 1), 0)
    inside = jnp.where((frames >= 0) & (frames < limit), 1.0, 0.0)
    projected = jnp.dot(ctx[0].reshape(48, HALF), wo[:HALF], preferred_element_type=F32) + jnp.dot(
        ctx[1].reshape(48, HALF), wo[HALF:], preferred_element_type=F32
    )
    mixed = res[...].reshape(48, 1024).astype(F32) + inside * projected
    average = jnp.mean(mixed, axis=-1, keepdims=True)
    centred = mixed - average
    variance = jnp.mean(centred * centred, axis=-1, keepdims=True)
    normed = (centred * lax.rsqrt(variance + 1e-05) * gain[...] + bias[...]).astype(BF16)
    lifted = jnp.dot(normed, wi[...], preferred_element_type=F32)
    gated[...] = (
        (inside * lifted[:, :512] * jax.nn.sigmoid(lifted[:, 512:])).astype(BF16).astype(F32)
    )
    filtered = taps[0:1, :] * gated[1 : 1 + ROWS, :]
    for tap in range(1, 31):
        filtered = filtered + taps[tap : tap + 1, :] * gated[tap + 1 : tap + 1 + ROWS, :]
    shifted = filtered * scale[...] + shift[...]
    activated = (shifted * jax.nn.sigmoid(shifted)).astype(BF16)
    out_ref[...] = (mixed[ROWS : 2 * ROWS] + jnp.dot(activated, wc[...], preferred_element_type=F32)).astype(BF16)

    for copy in first_copies + relay_copies + [q_first] + q_copies + [res_right, res_left] + a_copies + c_copies:
        copy.wait_send()


def on_device(
    queries, keys, values, residual, lengths, out_proj, ln_gain, ln_bias, conv_in, taps, bn_scale, bn_shift, conv_out
):
    hbm = pl.BlockSpec(memory_space=pl.ANY)
    dma = pltpu.SemaphoreType.DMA
    return pl.pallas_call(
        kernel,
        out_shape=jax.ShapeDtypeStruct((ROWS, 1024), BF16),
        in_specs=[hbm] * 4 + [pl.BlockSpec(memory_space=pltpu.SMEM)] + [hbm] * 8,
        out_specs=pl.BlockSpec(memory_space=pltpu.VMEM),
        scratch_shapes=[
            pltpu.VMEM((ROWS, 512), BF16),
            pltpu.VMEM((ROWS, 512), BF16),
            pltpu.VMEM((ROWS, 512), BF16),
            pltpu.VMEM((3, ROWS, 1024), BF16),
            pltpu.VMEM((512, 1024), BF16),
            pltpu.VMEM((1, 1024), F32),
            pltpu.VMEM((1, 1024), F32),
            pltpu.VMEM((1024, 1024), BF16),
            pltpu.VMEM((31, 512), F32),
            pltpu.VMEM((1, 512), F32),
            pltpu.VMEM((1, 512), F32),
            pltpu.VMEM((512, 1024), BF16),
            pltpu.VMEM((2, 2, ROWS, HALF), BF16),
            pltpu.VMEM((NZ, 2, ROWS, HALF), BF16),
            pltpu.VMEM((2, ROWS, HALF), BF16),
            pltpu.VMEM((SLAB, 2, ROWS, HALF), BF16),
            pltpu.VMEM((256, HALF + 128), BF16),
            pltpu.VMEM((SLAB, 32, HALF + 128), BF16),
            pltpu.VMEM((2, ROWS, HALF), BF16),
            pltpu.VMEM((2, 3, ROWS, HALF), BF16),
            pltpu.VMEM((48, 512), F32),
            dma((12,)),
            dma((NZ,)),
            dma((NZ,)),
            dma((SLAB,)),
            dma((SLAB,)),
            dma((2,)),
            dma((2,)),
            dma((SLAB,)),
            dma((SLAB,)),
            dma((2, 3)),
            dma((2, 3)),
        ],
        compiler_params=pltpu.CompilerParams(
            collective_id=0, has_side_effects=True, vmem_limit_bytes=40 * 1024 * 1024
        ),
        name="conformer",
    )(
        queries, keys, values, residual, lengths, out_proj, ln_gain.reshape(1, -1), ln_bias.reshape(1, -1), conv_in,
        taps, bn_scale.reshape(1, -1), bn_shift.reshape(1, -1), conv_out,
    )


def solution(mesh):
    rows = P(("dp", "seq"), None)
    return jax.shard_map(
        on_device,
        mesh=mesh,
        in_specs=(rows, rows, rows, rows, P("dp")) + (P(),) * 8,
        out_specs=rows,
        check_vma=False,
    )
```

```python
import functools
import math

import jax
import jax.numpy as jnp
from jax import lax
from jax.experimental import pallas as pl
from jax.experimental.pallas import tpu as pltpu
from jax.sharding import PartitionSpec as P

MESH = pl.DeviceIdType.MESH
BF16 = jnp.bfloat16
F32 = jnp.float32

NZ = 16
SLAB = 8
ROWS = 16
HALF = 256
HEAD = 64


def slot_of(offset):
    return 2 * abs(offset) - (1 if offset > 0 else 0)


FIRST = (4, -4, 3, -3)
NEAR = (2, -2, 1, -1)
RELAYS = ((-4, 4), (-3, 4), (3, -4), (-4, 2), (4, -2), (-3, 2), (3, -2))


def landed(offset):
    return 15 if offset in (8, -8) else slot_of(offset)


def kernel(
    q_hbm, k_hbm, v_hbm, res_hbm, len_ref, wo_hbm, gain_hbm, bias_hbm, wi_hbm, taps_hbm, scale_hbm, shift_hbm, wc_hbm,
    out_ref,
    q_in, k_in, v_in, res, wo, gain, bias, wi, taps, scale, shift, wc,
    kv_own, kv, q_own, q_all, a_send, a_recv, ctx_own, ctx, gated,
    in_sem, kv_ss, kv_rs, q_ss, q_rs, r_ss, r_rs, a_ss, a_rs, c_ss, c_rs,
):
    me = lax.axis_index("seq")
    z = me // SLAB
    xc = lax.rem(me, SLAB)
    par = lax.rem(z, 2)
    other = 1 - par
    limit = len_ref[0]

    def at_z(offset):
        return lax.rem(z + offset + NZ, NZ) * SLAB + xc

    def at_slab(step):
        return z * SLAB + lax.rem(xc + step, SLAB)

    partner = (z + 1 - 2 * par) * SLAB + xc
    left = lax.rem(me + 127, 128)
    right = lax.rem(me + 1, 128)

    loads = [
        pltpu.make_async_copy(src, dst, in_sem.at[i])
        for i, (src, dst) in enumerate(
            (
                (k_hbm, k_in), (v_hbm, v_in), (q_hbm, q_in), (res_hbm, res.at[1]),
                (wo_hbm, wo), (wi_hbm, wi), (wc_hbm, wc),
                (gain_hbm, gain), (bias_hbm, bias), (taps_hbm, taps), (scale_hbm, scale), (shift_hbm, shift),
            )
        )
    ]
    for load in loads[:4]:
        load.start()

    barrier = pltpu.get_barrier_semaphore()
    greet = [at_z(d) for d in FIRST + NEAR] + [at_slab(i) for i in range(1, SLAB)] + [left, right]
    for target in greet:
        pl.semaphore_signal(barrier, inc=1, device_id={"seq": target}, device_id_type=MESH)
    for load in loads[4:]:
        load.start()
    for load in loads[:3]:
        load.wait()
    for g in range(2):
        kv_own[g, 0] = k_in[:, HALF * g : HALF * (g + 1)]
        kv_own[g, 1] = v_in[:, HALF * g : HALF * (g + 1)]
        q_own[g] = q_in[:, HALF * g : HALF * (g + 1)]
    kv[0] = kv_own[par]
    q_all[xc, par] = q_own[par]
    loads[3].wait()
    pl.semaphore_wait(barrier, len(greet))

    def remote(src, dst, ss, rs, target):
        return pltpu.make_async_remote_copy(
            src_ref=src, dst_ref=dst, send_sem=ss, recv_sem=rs, device_id={"seq": target}, device_id_type=MESH
        )

    def first(d):
        slot = slot_of(-d)
        g = lax.rem(par + abs(d), 2)
        return remote(kv_own.at[g], kv.at[slot], kv_ss.at[slot], kv_rs.at[slot], at_z(d))

    def relay(source, d):
        slot = landed(source - d)
        return remote(kv.at[slot_of(source)], kv.at[slot], kv_ss.at[slot], kv_rs.at[slot], at_z(d))

    def arrived(slot):
        remote(kv.at[slot], kv.at[slot], kv_ss.at[slot], kv_rs.at[slot], right).wait_recv()

    first_copies = [first(d) for d in FIRST + NEAR]
    q_first = remote(q_own.at[other], q_all.at[xc, par], q_ss.at[0], q_rs.at[0], partner)
    for copy in first_copies[:4]:
        copy.start()
    q_first.start()
    for copy in first_copies[4:]:
        copy.start()

    remote(q_own.at[other], q_all.at[xc, other], q_ss.at[0], q_rs.at[0], partner).wait_recv()
    q_copies = [
        remote(q_all.at[xc], q_all.at[xc], q_ss.at[i], q_rs.at[i], at_slab(i)) for i in range(1, SLAB)
    ]
    for copy in q_copies:
        copy.start()
    res_right = remote(res.at[1], res.at[0], r_ss.at[0], r_rs.at[0], right)
    res_left = remote(res.at[1], res.at[2], r_ss.at[1], r_rs.at[1], left)
    res_right.start()
    res_left.start()

    relay_copies = []
    seen = []
    for source, d in RELAYS:
        if source not in seen:
            arrived(slot_of(source))
            seen.append(source)
        copy = relay(source, d)
        copy.start()
        relay_copies.append(copy)

    for i in range(1, SLAB):
        sender = lax.rem(xc + SLAB - i, SLAB)
        remote(q_all.at[sender], q_all.at[sender], q_ss.at[i], q_rs.at[i], at_slab(i)).wait_recv()
    for offset in (1, -1, 2, -2):
        arrived(slot_of(offset))

    lane = lax.broadcasted_iota(jnp.int32, (1, 128), 1)
    low = lane < HEAD
    factor = 1.0 / math.sqrt(HEAD)

    queries = []
    for pair in range(2):
        tile = q_all[:, :, :, 128 * pair : 128 * (pair + 1)].reshape(256, 128) * jnp.asarray(factor, BF16)
        zero = jnp.zeros_like(tile)
        queries.append((jnp.where(low, tile, zero), jnp.where(low, zero, tile)))

    def chunk(part):
        slot = 8 * part + lane // ROWS
        away = (slot + 1) // 2
        offset = jnp.where(lax.rem(slot, 2) == 1, away, -away)
        source = lax.rem(z + offset + NZ, NZ)
        frame = (source * SLAB + xc) * ROWS + lax.rem(lane, ROWS)
        valid = frame < limit
        result = []
        for pair in range(2):
            cols = slice(128 * pair, 128 * (pair + 1))
            key = kv[8 * part : 8 * part + 8, 0, :, cols].reshape(128, 128)
            value = kv[8 * part : 8 * part + 8, 1, :, cols].reshape(128, 128)
            for half in range(2):
                scores = lax.dot_general(
                    queries[pair][half], key, (((1,), (1,)), ((), ())), preferred_element_type=F32
                )
                scores = jnp.where(valid, scores, -1e30)
                top = jnp.max(scores, axis=-1, keepdims=True)
                powered = jnp.exp(scores - top)
                total = jnp.sum(powered, axis=-1, keepdims=True)
                mixed_values = jnp.dot(powered.astype(BF16), value, preferred_element_type=F32)
                result.append((top, total, mixed_values))
        return result

    near = chunk(0)
    arrived(slot_of(-4)) if -4 not in seen else None
    for slot in range(9, 16):
        arrived(slot)
    far = chunk(1)

    stats = jnp.zeros((256, 128), F32)
    for pair in range(2):
        tiles = []
        for half in range(2):
            head = 2 * pair + half
            top_a, total_a, mixed_a = near[head]
            top_b, total_b, mixed_b = far[head]
            top = jnp.maximum(top_a, top_b)
            grow_a = jnp.exp(top_a - top)
            grow_b = jnp.exp(top_b - top)
            total = grow_a * total_a + grow_b * total_b
            inverse = 1.0 / total
            tiles.append((grow_a * inverse) * mixed_a + (grow_b * inverse) * mixed_b)
            level = top + jnp.log(total)
            for step in range(3):
                rounded = level.astype(BF16).astype(F32)
                stats = jnp.where(lane == 3 * head + step, rounded, stats)
                level = level - rounded
        a_send[:, 128 * pair : 128 * (pair + 1)] = jnp.where(low, tiles[0], tiles[1]).astype(BF16)
    a_send[:, HALF : HALF + 128] = stats.astype(BF16)

    a_copies = []
    for i in range(1, SLAB):
        owner = lax.rem(xc + i, SLAB)
        copy = remote(
            a_send.at[pl.ds(pl.multiple_of(owner * 32, 32), 32)], a_recv.at[xc], a_ss.at[i], a_rs.at[i], at_slab(i)
        )
        copy.start()
        a_copies.append(copy)
    a_recv[xc] = a_send[pl.ds(pl.multiple_of(xc * 32, 32), 32), :]
    row_id = lax.broadcasted_iota(jnp.int32, (128, HALF), 0)
    col_id = lax.broadcasted_iota(jnp.int32, (128, HALF), 1)
    spread = jnp.where(row_id // 3 == col_id // HEAD, 1.0, 0.0).astype(BF16)
    for i in range(1, SLAB):
        sender = lax.rem(xc + SLAB - i, SLAB)
        remote(a_recv.at[sender], a_recv.at[sender], a_ss.at[i], a_rs.at[i], at_slab(i)).wait_recv()
    parts = a_recv[:, :, :HALF].astype(F32)
    levels = jnp.dot(
        a_recv[:, :, HALF : HALF + 128].reshape(256, 128), spread, preferred_element_type=F32
    ).reshape(8, 32, HALF)
    weights = jnp.exp(levels - jnp.max(levels, axis=0, keepdims=True))
    context = jnp.sum(weights * parts, axis=0) / jnp.sum(weights, axis=0)
    ctx_own[...] = context.astype(BF16).reshape(2, ROWS, HALF)

    c_copies = []
    for where, (slab, start) in enumerate(((par, me), (other, partner))):
        for place, shift_by in ((0, 1), (2, 127), (1, 0)):
            if where == 0 and place == 1:
                continue
            target = lax.rem(start + shift_by, 128)
            copy = remote(
                ctx_own.at[slab], ctx.at[par, place], c_ss.at[where, place], c_rs.at[par, place], target
            )
            copy.start()
            c_copies.append(copy)
    ctx[par, 1] = ctx_own[par]

    for load in loads[4:]:
        load.wait()
    for place in (0, 2):
        for g in range(2):
            remote(ctx.at[g, place], ctx.at[g, place], c_ss.at[0, place], c_rs.at[g, place], right).wait_recv()
    remote(ctx.at[other, 1], ctx.at[other, 1], c_ss.at[1, 1], c_rs.at[other, 1], right).wait_recv()
    remote(res.at[1], res.at[0], r_ss.at[0], r_rs.at[0], right).wait_recv()
    remote(res.at[1], res.at[2], r_ss.at[1], r_rs.at[1], left).wait_recv()

    frames = (me - 1) * ROWS + lax.broadcasted_iota(jnp.int32, (48, 1), 0)
    inside = jnp.where((frames >= 0) & (frames < limit), 1.0, 0.0)
    projected = jnp.dot(ctx[0].reshape(48, HALF), wo[:HALF], preferred_element_type=F32) + jnp.dot(
        ctx[1].reshape(48, HALF), wo[HALF:], preferred_element_type=F32
    )
    mixed = res[...].reshape(48, 1024).astype(F32) + inside * projected
    average = jnp.mean(mixed, axis=-1, keepdims=True)
    centred = mixed - average
    variance = jnp.mean(centred * centred, axis=-1, keepdims=True)
    normed = (centred * lax.rsqrt(variance + 1e-05) * gain[...] + bias[...]).astype(BF16)
    lifted = jnp.dot(normed, wi[...], preferred_element_type=F32)
    gated[...] = (
        (inside * lifted[:, :512] * jax.nn.sigmoid(lifted[:, 512:])).astype(BF16).astype(F32)
    )
    filtered = taps[0:1, :] * gated[1 : 1 + ROWS, :]
    for tap in range(1, 31):
        filtered = filtered + taps[tap : tap + 1, :] * gated[tap + 1 : tap + 1 + ROWS, :]
    shifted = filtered * scale[...] + shift[...]
    activated = (shifted * jax.nn.sigmoid(shifted)).astype(BF16)
    out_ref[...] = (mixed[ROWS : 2 * ROWS] + jnp.dot(activated, wc[...], preferred_element_type=F32)).astype(BF16)

    for copy in first_copies + relay_copies + [q_first] + q_copies + [res_right, res_left] + a_copies + c_copies:
        copy.wait_send()


def on_device(
    queries, keys, values, residual, lengths, out_proj, ln_gain, ln_bias, conv_in, taps, bn_scale, bn_shift, conv_out
):
    hbm = pl.BlockSpec(memory_space=pltpu.HBM)
    dma = pltpu.SemaphoreType.DMA
    return pl.pallas_call(
        kernel,
        out_shape=jax.ShapeDtypeStruct((ROWS, 1024), BF16),
        in_specs=[hbm] * 4 + [pl.BlockSpec(memory_space=pltpu.SMEM)] + [hbm] * 8,
        out_specs=pl.BlockSpec(memory_space=pltpu.VMEM),
        scratch_shapes=[
            pltpu.VMEM((ROWS, 512), BF16),
            pltpu.VMEM((ROWS, 512), BF16),
            pltpu.VMEM((ROWS, 512), BF16),
            pltpu.VMEM((3, ROWS, 1024), BF16),
            pltpu.VMEM((512, 1024), BF16),
            pltpu.VMEM((1, 1024), F32),
            pltpu.VMEM((1, 1024), F32),
            pltpu.VMEM((1024, 1024), BF16),
            pltpu.VMEM((31, 512), F32),
            pltpu.VMEM((1, 512), F32),
            pltpu.VMEM((1, 512), F32),
            pltpu.VMEM((512, 1024), BF16),
            pltpu.VMEM((2, 2, ROWS, HALF), BF16),
            pltpu.VMEM((NZ, 2, ROWS, HALF), BF16),
            pltpu.VMEM((2, ROWS, HALF), BF16),
            pltpu.VMEM((SLAB, 2, ROWS, HALF), BF16),
            pltpu.VMEM((256, HALF + 128), BF16),
            pltpu.VMEM((SLAB, 32, HALF + 128), BF16),
            pltpu.VMEM((2, ROWS, HALF), BF16),
            pltpu.VMEM((2, 3, ROWS, HALF), BF16),
            pltpu.VMEM((48, 512), F32),
            dma((12,)),
            dma((NZ,)),
            dma((NZ,)),
            dma((SLAB,)),
            dma((SLAB,)),
            dma((2,)),
            dma((2,)),
            dma((SLAB,)),
            dma((SLAB,)),
            dma((2, 3)),
            dma((2, 3)),
        ],
        compiler_params=pltpu.CompilerParams(
            collective_id=0, has_side_effects=True, vmem_limit_bytes=40 * 1024 * 1024
        ),
        name="conformer",
    )(
        *[pltpu.with_memory_space_constraint(a, pltpu.HBM) if a is not lengths else a for a in (queries, keys, values, residual, lengths, out_proj, ln_gain.reshape(1, -1), ln_bias.reshape(1, -1), conv_in,
        taps, bn_scale.reshape(1, -1), bn_shift.reshape(1, -1), conv_out)],
    )


def solution(mesh):
    rows = P(("dp", "seq"), None)
    return jax.shard_map(
        on_device,
        mesh=mesh,
        in_specs=(rows, rows, rows, rows, P("dp")) + (P(),) * 8,
        out_specs=rows,
        check_vma=False,
    )
```

```python
import math

import jax
import jax.numpy as jnp
from jax import lax
from jax.experimental import pallas as pl
from jax.experimental.pallas import tpu as pltpu
from jax.sharding import PartitionSpec as P

MESH = pl.DeviceIdType.MESH
BF16 = jnp.bfloat16
F32 = jnp.float32

NZ = 16
SLAB = 8
ROWS = 16
WIDE = 128
HEAD = 64


def slot_of(offset):
    return 15 if offset in (8, -8) else 2 * abs(offset) - (1 if offset > 0 else 0)


FIRST = (4, -4, 3, -3, 2, -2, 1, -1)
RELAYS = ((-1, 4), (1, -4), (-2, 4), (2, -4), (-3, 4), (3, -4), (-4, 4))


def kernel(
    q_hbm, k_hbm, v_hbm, res_hbm, len_ref, wo_hbm, gain_hbm, bias_hbm, wi_hbm, taps_hbm, scale_hbm, shift_hbm, wc_hbm,
    out_ref,
    q_in, k_in, v_in, res, wo, gain, bias, wi, taps, scale, shift, wc,
    kv_own, kv, q_own, q_all, a_send, a_recv, ctx_own, ctx, gated,
    in_sem, kv_ss, kv_rs, q_ss, q_rs, r_ss, r_rs, a_ss, a_rs, c_ss, c_rs,
):
    me = lax.axis_index("seq")
    z = me // SLAB
    xc = lax.rem(me, SLAB)
    mine = lax.rem(z + 1, 4)
    limit = len_ref[0]

    def at_z(offset):
        return lax.rem(z + offset + NZ, NZ) * SLAB + xc

    def at_slab(step):
        return z * SLAB + lax.rem(xc + step, SLAB)

    def member(place):
        return lax.rem(z - mine + place + NZ, NZ)

    has_left = me != 0
    has_right = me != 127
    left = jnp.maximum(me - 1, 0)
    right = jnp.minimum(me + 1, 127)
    slab_steps = (4, 3, 5, 2, 6, 7, 1)

    barrier = pltpu.get_barrier_semaphore()

    def greet(target):
        pl.semaphore_signal(barrier, inc=1, device_id={"seq": target}, device_id_type=MESH)

    for d in FIRST[:6]:
        greet(at_z(d))
    for step in slab_steps:
        greet(at_slab(step))
    for d in FIRST[6:]:
        greet(at_z(d))

    loads = [
        pltpu.make_async_copy(src, dst, in_sem.at[i])
        for i, (src, dst) in enumerate(
            (
                (k_hbm, k_in), (v_hbm, v_in), (q_hbm, q_in), (res_hbm, res.at[1]),
                (wo_hbm, wo), (wi_hbm, wi), (wc_hbm, wc),
                (gain_hbm, gain), (bias_hbm, bias), (taps_hbm, taps), (scale_hbm, scale), (shift_hbm, shift),
            )
        )
    ]
    for load in loads:
        load.start()
    for load in loads[:3]:
        load.wait()
    for g in range(4):
        cols = slice(WIDE * g, WIDE * (g + 1))
        kv_own[g, 0] = k_in[:, cols]
        kv_own[g, 1] = v_in[:, cols]
        q_own[g] = q_in[:, cols]
    kv[0] = kv_own[mine]
    q_all[xc, mine] = q_own[mine]
    loads[3].wait()
    pl.semaphore_wait(barrier, 15)

    def remote(src, dst, ss, rs, target):
        return pltpu.make_async_remote_copy(
            src_ref=src, dst_ref=dst, send_sem=ss, recv_sem=rs, device_id={"seq": target}, device_id_type=MESH
        )

    def first(d):
        slot = slot_of(-d)
        return remote(
            kv_own.at[lax.rem(mine + d + 4, 4)], kv.at[slot], kv_ss.at[slot], kv_rs.at[slot], at_z(d)
        )

    def relay(source, d):
        slot = slot_of(source - d)
        return remote(kv.at[slot_of(source)], kv.at[slot], kv_ss.at[slot], kv_rs.at[slot], at_z(d))

    def arrived(slot):
        remote(kv.at[slot], kv.at[slot], kv_ss.at[slot], kv_rs.at[slot], right).wait_recv()

    sent = []

    def start(copy):
        copy.start()
        sent.append(copy)

    for d in FIRST[:4]:
        start(first(d))
    for turn in (2, 1, 3):
        place = lax.rem(mine + turn, 4)
        start(
            remote(
                q_own.at[place], q_all.at[xc, mine], q_ss.at[turn], q_rs.at[turn], member(place) * SLAB + xc
            )
        )
    for d in FIRST[4:]:
        start(first(d))
    for source, d in RELAYS[:2]:
        arrived(slot_of(source))
        start(relay(source, d))
    for turn in (2, 1, 3):
        place = lax.rem(mine + 4 - turn, 4)
        remote(q_own.at[0], q_all.at[xc, place], q_ss.at[turn], q_rs.at[turn], right).wait_recv()
    for step in slab_steps:
        start(remote(q_all.at[xc], q_all.at[xc], q_ss.at[4 + step], q_rs.at[4 + step], at_slab(step)))

    for source, d in RELAYS[2:]:
        arrived(slot_of(source))
        start(relay(source, d))

    for step in slab_steps:
        sender = lax.rem(xc + SLAB - step, SLAB)
        remote(q_all.at[sender], q_all.at[sender], q_ss.at[4 + step], q_rs.at[4 + step], right).wait_recv()
    res_right = remote(res.at[1], res.at[0], r_ss.at[0], r_rs.at[0], right)
    res_left = remote(res.at[1], res.at[2], r_ss.at[1], r_rs.at[1], left)
    pl.when(has_right)(res_right.start)
    pl.when(has_left)(res_left.start)
    arrived(slot_of(4))

    lane = lax.broadcasted_iota(jnp.int32, (1, WIDE), 1)
    low = lane < HEAD
    tile = q_all[...].reshape(512, WIDE) * jnp.asarray(1.0 / math.sqrt(HEAD), BF16)
    zero = jnp.zeros_like(tile)
    queries = (jnp.where(low, tile, zero), jnp.where(low, zero, tile))

    def chunk(part):
        slot = 8 * part + lane // ROWS
        away = (slot + 1) // 2
        offset = jnp.where(lax.rem(slot, 2) == 1, away, -away)
        source = lax.rem(z + offset + NZ, NZ)
        frame = (source * SLAB + xc) * ROWS + lax.rem(lane, ROWS)
        valid = frame < limit
        key = kv[8 * part : 8 * part + 8, 0].reshape(128, WIDE)
        value = kv[8 * part : 8 * part + 8, 1].reshape(128, WIDE)
        result = []
        for half in range(2):
            scores = lax.dot_general(queries[half], key, (((1,), (1,)), ((), ())), preferred_element_type=F32)
            scores = jnp.where(valid, scores, -1e30)
            top = jnp.max(scores, axis=-1, keepdims=True)
            powered = jnp.exp(scores - top)
            total = jnp.sum(powered, axis=-1, keepdims=True)
            result.append((top, total, jnp.dot(powered.astype(BF16), value, preferred_element_type=F32)))
        return result

    near = chunk(0)
    for slot in range(9, 16):
        arrived(slot)
    far = chunk(1)

    home = 8 * lax.rem(lax.broadcasted_iota(jnp.int32, (512, WIDE), 0) // ROWS, 4)
    wide_lane = lax.broadcasted_iota(jnp.int32, (512, WIDE), 1) - home
    stats = jnp.zeros((512, WIDE), F32)
    tiles = []
    for half in range(2):
        top_a, total_a, values_a = near[half]
        top_b, total_b, values_b = far[half]
        top = jnp.maximum(top_a, top_b)
        grow_a = jnp.exp(top_a - top)
        grow_b = jnp.exp(top_b - top)
        total = grow_a * total_a + grow_b * total_b
        inverse = 1.0 / total
        tiles.append((grow_a * inverse) * values_a + (grow_b * inverse) * values_b)
        level = top + jnp.log(total)
        for step in range(3):
            rounded = level.astype(BF16).astype(F32)
            stats = jnp.where(wide_lane == 3 * half + step, rounded, stats)
            level = level - rounded
    a_send[:, :64] = jnp.where(low, tiles[0], tiles[1]).astype(BF16).reshape(SLAB, 64, WIDE)
    a_send[:, 64:] = jnp.sum(stats.reshape(SLAB, 4, ROWS, WIDE), axis=1).astype(BF16)

    for step in slab_steps:
        owner = lax.rem(xc + step, SLAB)
        start(remote(a_send.at[owner], a_recv.at[xc], a_ss.at[step], a_rs.at[step], at_slab(step)))
    a_recv[xc] = a_send[xc]
    row_id = lax.broadcasted_iota(jnp.int32, (WIDE, WIDE), 0)
    col_id = lax.broadcasted_iota(jnp.int32, (WIDE, WIDE), 1)
    part_id = lax.rem(row_id, 8)
    picks = [
        jnp.where(
            (row_id // 8 == g) & (part_id >= 3 * (col_id // HEAD)) & (part_id < 3 * (col_id // HEAD) + 3), 1.0, 0.0
        ).astype(BF16)
        for g in range(4)
    ]
    for step in slab_steps[::-1]:
        sender = lax.rem(xc + SLAB - step, SLAB)
        remote(a_recv.at[sender], a_recv.at[sender], a_ss.at[step], a_rs.at[step], right).wait_recv()
    packed = a_recv[:, 64:].reshape(SLAB * ROWS, WIDE)
    for g in range(4):
        levels = jnp.dot(packed, picks[g], preferred_element_type=F32).reshape(SLAB, ROWS, WIDE)
        weights = jnp.exp(levels - jnp.max(levels, axis=0, keepdims=True))
        parts = a_recv[:, ROWS * g : ROWS * (g + 1)].astype(F32)
        ctx_own[g] = (jnp.sum(weights * parts, axis=0) / jnp.sum(weights, axis=0)).astype(BF16)

    edges = []
    for slab in (1, 2, 3, 0):
        home_device = member(slab) * SLAB + xc
        for place in (0, 2, 1):
            target = home_device + 1 - place
            if place == 1:
                exists = slab != mine
                target = home_device
            else:
                exists = (target >= 0) & (target < 128)
            copy = remote(
                ctx_own.at[slab], ctx.at[mine, place], c_ss.at[slab, place], c_rs.at[mine, place],
                jnp.clip(target, 0, 127),
            )
            pl.when(exists)(copy.start)
            edges.append((exists, copy))
    ctx[mine, 1] = ctx_own[mine]

    for load in loads[4:]:
        load.wait()
    def ctx_arrived(group, place):
        remote(ctx.at[group, place], ctx.at[group, place], c_ss.at[0, 0], c_rs.at[group, place], right).wait_recv()

    for turn in range(1, 4):
        ctx_arrived(lax.rem(mine + turn, 4), 1)

    def receive_edge(place):
        for group in range(4):
            ctx_arrived(group, place)

    def blank(place):
        res[place] = jnp.zeros((ROWS, 1024), BF16)
        for group in range(4):
            ctx[group, place] = jnp.zeros((ROWS, WIDE), BF16)

    pl.when(has_left)(remote(res.at[1], res.at[0], r_ss.at[0], r_rs.at[0], right).wait_recv)
    pl.when(has_right)(remote(res.at[1], res.at[2], r_ss.at[1], r_rs.at[1], left).wait_recv)
    pl.when(has_left)(lambda: receive_edge(0))
    pl.when(has_right)(lambda: receive_edge(2))
    pl.when(jnp.logical_not(has_left))(lambda: blank(0))
    pl.when(jnp.logical_not(has_right))(lambda: blank(2))

    frames = (me - 1) * ROWS + lax.broadcasted_iota(jnp.int32, (48, 1), 0)
    inside = jnp.where((frames >= 0) & (frames < limit), 1.0, 0.0)
    context = jnp.concatenate([ctx[group].reshape(48, WIDE) for group in range(4)], axis=1)
    projected = jnp.dot(context, wo[...], preferred_element_type=F32)
    mixed = res[...].reshape(48, 1024).astype(F32) + inside * projected
    average = jnp.mean(mixed, axis=-1, keepdims=True)
    centred = mixed - average
    variance = jnp.mean(centred * centred, axis=-1, keepdims=True)
    normed = (centred * lax.rsqrt(variance + 1e-05) * gain[...] + bias[...]).astype(BF16)
    lifted = jnp.dot(normed, wi[...], preferred_element_type=F32)
    gated[...] = (inside * lifted[:, :512] * jax.nn.sigmoid(lifted[:, 512:])).astype(BF16).astype(F32)
    filtered = taps[0:1, :] * gated[1 : 1 + ROWS, :]
    for tap in range(1, 31):
        filtered = filtered + taps[tap : tap + 1, :] * gated[tap + 1 : tap + 1 + ROWS, :]
    shifted = filtered * scale[...] + shift[...]
    activated = (shifted * jax.nn.sigmoid(shifted)).astype(BF16)
    out_ref[...] = (mixed[ROWS : 2 * ROWS] + jnp.dot(activated, wc[...], preferred_element_type=F32)).astype(BF16)

    for copy in sent:
        copy.wait_send()
    pl.when(has_right)(res_right.wait_send)
    pl.when(has_left)(res_left.wait_send)
    for exists, copy in edges:
        pl.when(exists)(copy.wait_send)


def on_device(
    queries, keys, values, residual, lengths, out_proj, ln_gain, ln_bias, conv_in, taps, bn_scale, bn_shift, conv_out
):
    hbm = pl.BlockSpec(memory_space=pltpu.HBM)
    dma = pltpu.SemaphoreType.DMA

    def stay(array):
        return pltpu.with_memory_space_constraint(array, pltpu.HBM)

    def row(array):
        return stay(array.reshape(1, -1))

    return pl.pallas_call(
        kernel,
        out_shape=jax.ShapeDtypeStruct((ROWS, 1024), BF16),
        in_specs=[hbm] * 4 + [pl.BlockSpec(memory_space=pltpu.SMEM)] + [hbm] * 8,
        out_specs=pl.BlockSpec(memory_space=pltpu.VMEM),
        scratch_shapes=[
            pltpu.VMEM((ROWS, 512), BF16),
            pltpu.VMEM((ROWS, 512), BF16),
            pltpu.VMEM((ROWS, 512), BF16),
            pltpu.VMEM((3, ROWS, 1024), BF16),
            pltpu.VMEM((512, 1024), BF16),
            pltpu.VMEM((1, 1024), F32),
            pltpu.VMEM((1, 1024), F32),
            pltpu.VMEM((1024, 1024), BF16),
            pltpu.VMEM((31, 512), F32),
            pltpu.VMEM((1, 512), F32),
            pltpu.VMEM((1, 512), F32),
            pltpu.VMEM((512, 1024), BF16),
            pltpu.VMEM((4, 2, ROWS, WIDE), BF16),
            pltpu.VMEM((NZ, 2, ROWS, WIDE), BF16),
            pltpu.VMEM((4, ROWS, WIDE), BF16),
            pltpu.VMEM((SLAB, 4, ROWS, WIDE), BF16),
            pltpu.VMEM((SLAB, 80, WIDE), BF16),
            pltpu.VMEM((SLAB, 80, WIDE), BF16),
            pltpu.VMEM((4, ROWS, WIDE), BF16),
            pltpu.VMEM((4, 3, ROWS, WIDE), BF16),
            pltpu.VMEM((48, 512), F32),
            dma((12,)),
            dma((NZ,)),
            dma((NZ,)),
            dma((12,)),
            dma((12,)),
            dma((2,)),
            dma((2,)),
            dma((SLAB,)),
            dma((SLAB,)),
            dma((4, 3)),
            dma((4, 3)),
        ],
        compiler_params=pltpu.CompilerParams(
            collective_id=0, has_side_effects=True, vmem_limit_bytes=40 * 1024 * 1024
        ),
        name="conformer",
    )(
        stay(queries), stay(keys), stay(values), stay(residual), lengths, stay(out_proj), row(ln_gain), row(ln_bias),
        stay(conv_in), stay(taps), row(bn_scale), row(bn_shift), stay(conv_out),
    )


def solution(mesh):
    rows = P(("dp", "seq"), None)
    return jax.shard_map(
        on_device,
        mesh=mesh,
        in_specs=(rows, rows, rows, rows, P("dp")) + (P(),) * 8,
        out_specs=rows,
        check_vma=False,
    )
```

```python
import math

import jax
import jax.numpy as jnp
from jax import lax
from jax.experimental import pallas as pl
from jax.experimental.pallas import tpu as pltpu
from jax.sharding import PartitionSpec as P

MESH = pl.DeviceIdType.MESH
BF16 = jnp.bfloat16
F32 = jnp.float32

NZ = 16
SLAB = 8
ROWS = 16
WIDE = 128
HEAD = 64


def slot_of(offset):
    return 15 if offset in (8, -8) else 2 * abs(offset) - (1 if offset > 0 else 0)


FIRST = (4, -4, 3, -3, 2, -2, 1, -1)
RELAYS = ((-1, 4), (1, -4), (-2, 4), (2, -4), (-3, 4), (3, -4), (-4, 4))


def kernel(
    q_hbm, k_hbm, v_hbm, res_hbm, len_ref, wo_hbm, gain_hbm, bias_hbm, wi_hbm, taps_hbm, scale_hbm, shift_hbm, wc_hbm,
    out_ref,
    q_in, k_in, v_in, res, wo, gain, bias, wi, taps, scale, shift, wc,
    kv_own, kv, q_own, q_all, a_send, a_recv, ctx_own, ctx, gated,
    in_sem, kv_ss, kv_rs, q_ss, q_rs, r_ss, r_rs, a_ss, a_rs, c_ss, c_rs,
):
    me = lax.axis_index("seq")
    z = me // SLAB
    xc = lax.rem(me, SLAB)
    mine = lax.rem(z + 1, 4)
    limit = len_ref[0]

    def at_z(offset):
        return lax.rem(z + offset + NZ, NZ) * SLAB + xc

    def at_slab(step):
        return z * SLAB + lax.rem(xc + step, SLAB)

    def member(place):
        return lax.rem(z - mine + place + NZ, NZ)

    has_left = me != 0
    has_right = me != 127
    left = jnp.maximum(me - 1, 0)
    right = jnp.minimum(me + 1, 127)
    slab_steps = (4, 3, 5, 2, 6, 7, 1)

    barrier = pltpu.get_barrier_semaphore()

    def greet(target):
        pl.semaphore_signal(barrier, inc=1, device_id={"seq": target}, device_id_type=MESH)

    for d in FIRST[:6]:
        greet(at_z(d))
    for step in slab_steps:
        greet(at_slab(step))
    for d in FIRST[6:]:
        greet(at_z(d))

    loads = [
        pltpu.make_async_copy(src, dst, in_sem.at[i])
        for i, (src, dst) in enumerate(
            (
                (k_hbm, k_in), (v_hbm, v_in), (q_hbm, q_in), (res_hbm, res.at[1]),
                (wo_hbm, wo), (wi_hbm, wi), (wc_hbm, wc),
                (gain_hbm, gain), (bias_hbm, bias), (taps_hbm, taps), (scale_hbm, scale), (shift_hbm, shift),
            )
        )
    ]
    for load in loads:
        load.start()
    for load in loads[:3]:
        load.wait()
    for g in range(4):
        cols = slice(WIDE * g, WIDE * (g + 1))
        kv_own[g, 0] = k_in[:, cols]
        kv_own[g, 1] = v_in[:, cols]
        q_own[g] = q_in[:, cols]
    kv[0] = kv_own[mine]
    q_all[xc, mine] = q_own[mine]
    loads[3].wait()
    pl.semaphore_wait(barrier, 15)

    def remote(src, dst, ss, rs, target):
        return pltpu.make_async_remote_copy(
            src_ref=src, dst_ref=dst, send_sem=ss, recv_sem=rs, device_id={"seq": target}, device_id_type=MESH
        )

    def first(d):
        slot = slot_of(-d)
        return remote(
            kv_own.at[lax.rem(mine + d + 4, 4)], kv.at[slot], kv_ss.at[slot], kv_rs.at[slot], at_z(d)
        )

    def relay(source, d):
        slot = slot_of(source - d)
        return remote(kv.at[slot_of(source)], kv.at[slot], kv_ss.at[slot], kv_rs.at[slot], at_z(d))

    def arrived(slot):
        remote(kv.at[slot], kv.at[slot], kv_ss.at[slot], kv_rs.at[slot], right).wait_recv()

    sent = []

    def start(copy):
        copy.start()
        sent.append(copy)

    for turn in (2, 1, 3):
        place = lax.rem(mine + turn, 4)
        start(
            remote(
                q_own.at[place], q_all.at[xc, mine], q_ss.at[turn], q_rs.at[turn], member(place) * SLAB + xc
            )
        )
    for d in FIRST:
        start(first(d))
    for source, d in RELAYS[:4]:
        arrived(slot_of(source))
        start(relay(source, d))
    for turn in (2, 1, 3):
        place = lax.rem(mine + 4 - turn, 4)
        remote(q_own.at[0], q_all.at[xc, place], q_ss.at[turn], q_rs.at[turn], right).wait_recv()
    for step in slab_steps:
        start(remote(q_all.at[xc], q_all.at[xc], q_ss.at[4 + step], q_rs.at[4 + step], at_slab(step)))

    for source, d in RELAYS[4:]:
        arrived(slot_of(source))
        start(relay(source, d))

    for step in slab_steps:
        sender = lax.rem(xc + SLAB - step, SLAB)
        remote(q_all.at[sender], q_all.at[sender], q_ss.at[4 + step], q_rs.at[4 + step], right).wait_recv()
    arrived(slot_of(4))

    lane = lax.broadcasted_iota(jnp.int32, (1, WIDE), 1)
    low = lane < HEAD
    tile = q_all[...].reshape(512, WIDE) * jnp.asarray(1.0 / math.sqrt(HEAD), BF16)
    zero = jnp.zeros_like(tile)
    queries = (jnp.where(low, tile, zero), jnp.where(low, zero, tile))

    def chunk(part):
        slot = 8 * part + lane // ROWS
        away = (slot + 1) // 2
        offset = jnp.where(lax.rem(slot, 2) == 1, away, -away)
        source = lax.rem(z + offset + NZ, NZ)
        frame = (source * SLAB + xc) * ROWS + lax.rem(lane, ROWS)
        valid = frame < limit
        key = kv[8 * part : 8 * part + 8, 0].reshape(128, WIDE)
        value = kv[8 * part : 8 * part + 8, 1].reshape(128, WIDE)
        one = jnp.ones_like(value)
        result = []
        for half in range(2):
            scores = lax.dot_general(queries[half], key, (((1,), (1,)), ((), ())), preferred_element_type=F32)
            scores = jnp.where(valid, scores, -1e30)
            top = jnp.max(scores, axis=-1, keepdims=True)
            powered = jnp.exp(scores - top).astype(BF16)
            summed = jnp.where(low, value, one) if half == 0 else jnp.where(low, one, value)
            result.append((top, jnp.dot(powered, summed, preferred_element_type=F32)))
        return result

    near = chunk(0)
    res_right = remote(res.at[1], res.at[0], r_ss.at[0], r_rs.at[0], right)
    res_left = remote(res.at[1], res.at[2], r_ss.at[1], r_rs.at[1], left)
    pl.when(has_right)(res_right.start)
    pl.when(has_left)(res_left.start)
    for slot in range(9, 16):
        arrived(slot)
    far = chunk(1)

    tops = []
    sums = []
    for half in range(2):
        top_a, sum_a = near[half]
        top_b, sum_b = far[half]
        top = jnp.maximum(top_a, top_b)
        tops.append(top)
        sums.append(jnp.exp(top_a - top) * sum_a + jnp.exp(top_b - top) * sum_b)
    total = pltpu.roll(jnp.where(low, sums[1], sums[0]), HEAD, 1)
    a_send[:, :64] = (jnp.where(low, sums[0], sums[1]) / total).astype(BF16).reshape(SLAB, 64, WIDE)
    level = jnp.where(low, tops[0], tops[1]) + jnp.log(total)
    block = lax.rem(lax.broadcasted_iota(jnp.int32, (512, WIDE), 0) // ROWS, 4)
    place_of = lax.rem(lax.broadcasted_iota(jnp.int32, (512, WIDE), 1), HEAD) - 8 * block
    stats = jnp.zeros((512, WIDE), F32)
    for step in range(3):
        rounded = level.astype(BF16).astype(F32)
        stats = jnp.where(place_of == step, rounded, stats)
        level = level - rounded
    a_send[:, 64:] = jnp.sum(stats.reshape(SLAB, 4, ROWS, WIDE), axis=1).astype(BF16)

    for step in slab_steps:
        owner = lax.rem(xc + step, SLAB)
        start(remote(a_send.at[owner], a_recv.at[xc], a_ss.at[step], a_rs.at[step], at_slab(step)))
    a_recv[xc] = a_send[xc]
    row_id = lax.broadcasted_iota(jnp.int32, (WIDE, WIDE), 0)
    col_id = lax.broadcasted_iota(jnp.int32, (WIDE, WIDE), 1)
    same_half = (row_id // HEAD == col_id // HEAD) & (lax.rem(row_id, 8) < 3)
    picks = [
        jnp.where(same_half & (lax.rem(row_id, HEAD) // 8 == g), 1.0, 0.0).astype(BF16) for g in range(4)
    ]
    for step in slab_steps[::-1]:
        sender = lax.rem(xc + SLAB - step, SLAB)
        remote(a_recv.at[sender], a_recv.at[sender], a_ss.at[step], a_rs.at[step], right).wait_recv()
    packed = a_recv[:, 64:].reshape(SLAB * ROWS, WIDE)
    for g in range(4):
        levels = jnp.dot(packed, picks[g], preferred_element_type=F32).reshape(SLAB, ROWS, WIDE)
        weights = jnp.exp(levels - jnp.max(levels, axis=0, keepdims=True))
        parts = a_recv[:, ROWS * g : ROWS * (g + 1)].astype(F32)
        ctx_own[g] = (jnp.sum(weights * parts, axis=0) / jnp.sum(weights, axis=0)).astype(BF16)

    edges = []
    for slab in (1, 2, 3, 0):
        home_device = member(slab) * SLAB + xc
        for place in (0, 2, 1):
            target = home_device + 1 - place
            if place == 1:
                exists = slab != mine
                target = home_device
            else:
                exists = (target >= 0) & (target < 128)
            copy = remote(
                ctx_own.at[slab], ctx.at[mine, place], c_ss.at[slab, place], c_rs.at[mine, place],
                jnp.clip(target, 0, 127),
            )
            pl.when(exists)(copy.start)
            edges.append((exists, copy))
    ctx[mine, 1] = ctx_own[mine]

    for load in loads[4:]:
        load.wait()
    def ctx_arrived(group, place):
        remote(ctx.at[group, place], ctx.at[group, place], c_ss.at[0, 0], c_rs.at[group, place], right).wait_recv()

    for turn in range(1, 4):
        ctx_arrived(lax.rem(mine + turn, 4), 1)

    def receive_edge(place):
        for group in range(4):
            ctx_arrived(group, place)

    def blank(place):
        res[place] = jnp.zeros((ROWS, 1024), BF16)
        for group in range(4):
            ctx[group, place] = jnp.zeros((ROWS, WIDE), BF16)

    pl.when(has_left)(remote(res.at[1], res.at[0], r_ss.at[0], r_rs.at[0], right).wait_recv)
    pl.when(has_right)(remote(res.at[1], res.at[2], r_ss.at[1], r_rs.at[1], left).wait_recv)
    pl.when(has_left)(lambda: receive_edge(0))
    pl.when(has_right)(lambda: receive_edge(2))
    pl.when(jnp.logical_not(has_left))(lambda: blank(0))
    pl.when(jnp.logical_not(has_right))(lambda: blank(2))

    frames = (me - 1) * ROWS + lax.broadcasted_iota(jnp.int32, (48, 1), 0)
    inside = jnp.where((frames >= 0) & (frames < limit), 1.0, 0.0)
    context = jnp.concatenate([ctx[group].reshape(48, WIDE) for group in range(4)], axis=1)
    projected = jnp.dot(context, wo[...], preferred_element_type=F32)
    mixed = res[...].reshape(48, 1024).astype(F32) + inside * projected
    average = jnp.mean(mixed, axis=-1, keepdims=True)
    centred = mixed - average
    variance = jnp.mean(centred * centred, axis=-1, keepdims=True)
    normed = (centred * lax.rsqrt(variance + 1e-05) * gain[...] + bias[...]).astype(BF16)
    lifted = jnp.dot(normed, wi[...], preferred_element_type=F32)
    gated[...] = (inside * lifted[:, :512] * jax.nn.sigmoid(lifted[:, 512:])).astype(BF16).astype(F32)
    filtered = taps[0:1, :] * gated[1 : 1 + ROWS, :]
    for tap in range(1, 31):
        filtered = filtered + taps[tap : tap + 1, :] * gated[tap + 1 : tap + 1 + ROWS, :]
    shifted = filtered * scale[...] + shift[...]
    activated = (shifted * jax.nn.sigmoid(shifted)).astype(BF16)
    out_ref[...] = (mixed[ROWS : 2 * ROWS] + jnp.dot(activated, wc[...], preferred_element_type=F32)).astype(BF16)

    for copy in sent:
        copy.wait_send()
    pl.when(has_right)(res_right.wait_send)
    pl.when(has_left)(res_left.wait_send)
    for exists, copy in edges:
        pl.when(exists)(copy.wait_send)


def on_device(
    queries, keys, values, residual, lengths, out_proj, ln_gain, ln_bias, conv_in, taps, bn_scale, bn_shift, conv_out
):
    hbm = pl.BlockSpec(memory_space=pltpu.HBM)
    dma = pltpu.SemaphoreType.DMA

    def stay(array):
        return pltpu.with_memory_space_constraint(array, pltpu.HBM)

    def row(array):
        return stay(array.reshape(1, -1))

    return pl.pallas_call(
        kernel,
        out_shape=jax.ShapeDtypeStruct((ROWS, 1024), BF16),
        in_specs=[hbm] * 4 + [pl.BlockSpec(memory_space=pltpu.SMEM)] + [hbm] * 8,
        out_specs=pl.BlockSpec(memory_space=pltpu.VMEM),
        scratch_shapes=[
            pltpu.VMEM((ROWS, 512), BF16),
            pltpu.VMEM((ROWS, 512), BF16),
            pltpu.VMEM((ROWS, 512), BF16),
            pltpu.VMEM((3, ROWS, 1024), BF16),
            pltpu.VMEM((512, 1024), BF16),
            pltpu.VMEM((1, 1024), F32),
            pltpu.VMEM((1, 1024), F32),
            pltpu.VMEM((1024, 1024), BF16),
            pltpu.VMEM((31, 512), F32),
            pltpu.VMEM((1, 512), F32),
            pltpu.VMEM((1, 512), F32),
            pltpu.VMEM((512, 1024), BF16),
            pltpu.VMEM((4, 2, ROWS, WIDE), BF16),
            pltpu.VMEM((NZ, 2, ROWS, WIDE), BF16),
            pltpu.VMEM((4, ROWS, WIDE), BF16),
            pltpu.VMEM((SLAB, 4, ROWS, WIDE), BF16),
            pltpu.VMEM((SLAB, 80, WIDE), BF16),
            pltpu.VMEM((SLAB, 80, WIDE), BF16),
            pltpu.VMEM((4, ROWS, WIDE), BF16),
            pltpu.VMEM((4, 3, ROWS, WIDE), BF16),
            pltpu.VMEM((48, 512), F32),
            dma((12,)),
            dma((NZ,)),
            dma((NZ,)),
            dma((12,)),
            dma((12,)),
            dma((2,)),
            dma((2,)),
            dma((SLAB,)),
            dma((SLAB,)),
            dma((4, 3)),
            dma((4, 3)),
        ],
        compiler_params=pltpu.CompilerParams(
            collective_id=0, has_side_effects=True, vmem_limit_bytes=40 * 1024 * 1024
        ),
        name="conformer",
    )(
        stay(queries), stay(keys), stay(values), stay(residual), lengths, stay(out_proj), row(ln_gain), row(ln_bias),
        stay(conv_in), stay(taps), row(bn_scale), row(bn_shift), stay(conv_out),
    )


def solution(mesh):
    rows = P(("dp", "seq"), None)
    return jax.shard_map(
        on_device,
        mesh=mesh,
        in_specs=(rows, rows, rows, rows, P("dp")) + (P(),) * 8,
        out_specs=rows,
        check_vma=False,
    )
```

```python
import math

import jax
import jax.numpy as jnp
from jax import lax
from jax.experimental import pallas as pl
from jax.experimental.pallas import tpu as pltpu
from jax.sharding import PartitionSpec as P

MESH = pl.DeviceIdType.MESH
BF16 = jnp.bfloat16
F32 = jnp.float32

NZ = 16
SLAB = 8
ROWS = 16
WIDE = 128
HEAD = 64


def slot_of(offset):
    return 15 if offset in (8, -8) else 2 * abs(offset) - (1 if offset > 0 else 0)


FIRST = (4, -4, 3, -3, 2, -2, 1, -1)
RELAYS = ((-1, 4), (1, -4), (-2, 4), (2, -4), (-3, 4), (3, -4), (-4, 4))


def kernel(
    q_hbm, k_hbm, v_hbm, res_hbm, len_ref, wo_hbm, gain_hbm, bias_hbm, wi_hbm, taps_hbm, scale_hbm, shift_hbm, wc_hbm,
    out_ref,
    q_in, k_in, v_in, res, wo, gain, bias, wi, taps, scale, shift, wc,
    kv_own, kv, q_own, q_all, a_send, a_recv, ctx_own, ctx, gated,
    in_sem, kv_ss, kv_rs, q_ss, q_rs, r_ss, r_rs, a_ss, a_rs, c_ss, c_rs,
):
    me = lax.axis_index("seq")
    z = me // SLAB
    xc = lax.rem(me, SLAB)
    mine = lax.rem(z + 1, 4)
    limit = len_ref[0]

    def at_z(offset):
        return lax.rem(z + offset + NZ, NZ) * SLAB + xc

    def at_slab(step):
        return z * SLAB + lax.rem(xc + step, SLAB)

    def member(place):
        return lax.rem(z - mine + place + NZ, NZ)

    has_left = me != 0
    has_right = me != 127
    left = jnp.maximum(me - 1, 0)
    right = jnp.minimum(me + 1, 127)
    slab_steps = (4, 3, 5, 2, 6, 7, 1)

    barrier = pltpu.get_barrier_semaphore()

    def greet(target):
        pl.semaphore_signal(barrier, inc=1, device_id={"seq": target}, device_id_type=MESH)

    for d in FIRST[:6]:
        greet(at_z(d))
    for step in slab_steps:
        greet(at_slab(step))
    for d in FIRST[6:]:
        greet(at_z(d))

    loads = [
        pltpu.make_async_copy(src, dst, in_sem.at[i])
        for i, (src, dst) in enumerate(
            (
                (k_hbm, k_in), (v_hbm, v_in), (q_hbm, q_in), (res_hbm, res.at[1]),
                (wo_hbm, wo), (wi_hbm, wi), (wc_hbm, wc),
                (gain_hbm, gain), (bias_hbm, bias), (taps_hbm, taps), (scale_hbm, scale), (shift_hbm, shift),
            )
        )
    ]
    for load in loads:
        load.start()
    for load in loads[:3]:
        load.wait()
    for g in range(4):
        cols = slice(WIDE * g, WIDE * (g + 1))
        kv_own[g, 0] = k_in[:, cols]
        kv_own[g, 1] = v_in[:, cols]
        q_own[g] = q_in[:, cols]
    kv[0] = kv_own[mine]
    q_all[xc, mine] = q_own[mine]
    loads[3].wait()
    pl.semaphore_wait(barrier, 15)

    def remote(src, dst, ss, rs, target):
        return pltpu.make_async_remote_copy(
            src_ref=src, dst_ref=dst, send_sem=ss, recv_sem=rs, device_id={"seq": target}, device_id_type=MESH
        )

    def first(d):
        slot = slot_of(-d)
        return remote(
            kv_own.at[lax.rem(mine + d + 4, 4)], kv.at[slot], kv_ss.at[slot], kv_rs.at[slot], at_z(d)
        )

    def relay(source, d):
        slot = slot_of(source - d)
        return remote(kv.at[slot_of(source)], kv.at[slot], kv_ss.at[slot], kv_rs.at[slot], at_z(d))

    def arrived(slot):
        remote(kv.at[slot], kv.at[slot], kv_ss.at[slot], kv_rs.at[slot], right).wait_recv()

    sent = []

    def start(copy):
        copy.start()
        sent.append(copy)

    for turn in (2, 1, 3):
        place = lax.rem(mine + turn, 4)
        start(
            remote(
                q_own.at[place], q_all.at[xc, mine], q_ss.at[turn], q_rs.at[turn], member(place) * SLAB + xc
            )
        )
    for d in FIRST:
        start(first(d))
    for source, d in RELAYS[:4]:
        arrived(slot_of(source))
        start(relay(source, d))
    for turn in (2, 1, 3):
        place = lax.rem(mine + 4 - turn, 4)
        remote(q_own.at[0], q_all.at[xc, place], q_ss.at[turn], q_rs.at[turn], right).wait_recv()
    for step in slab_steps:
        start(remote(q_all.at[xc], q_all.at[xc], q_ss.at[4 + step], q_rs.at[4 + step], at_slab(step)))

    for source, d in RELAYS[4:]:
        arrived(slot_of(source))
        start(relay(source, d))

    for step in slab_steps:
        sender = lax.rem(xc + SLAB - step, SLAB)
        remote(q_all.at[sender], q_all.at[sender], q_ss.at[4 + step], q_rs.at[4 + step], right).wait_recv()
    arrived(slot_of(4))

    lane = lax.broadcasted_iota(jnp.int32, (1, WIDE), 1)
    low = lane < HEAD
    tile = q_all[...].reshape(512, WIDE) * jnp.asarray(1.0 / math.sqrt(HEAD), BF16)
    zero = jnp.zeros_like(tile)
    queries = (jnp.where(low, tile, zero), jnp.where(low, zero, tile))

    def chunk(part):
        slot = 8 * part + lane // ROWS
        away = (slot + 1) // 2
        offset = jnp.where(lax.rem(slot, 2) == 1, away, -away)
        source = lax.rem(z + offset + NZ, NZ)
        frame = (source * SLAB + xc) * ROWS + lax.rem(lane, ROWS)
        valid = frame < limit
        key = kv[8 * part : 8 * part + 8, 0].reshape(128, WIDE)
        value = kv[8 * part : 8 * part + 8, 1].reshape(128, WIDE)
        one = jnp.ones_like(value)
        result = []
        for half in range(2):
            scores = lax.dot_general(queries[half], key, (((1,), (1,)), ((), ())), preferred_element_type=F32)
            scores = jnp.where(valid, scores, -1e30)
            top = jnp.max(scores, axis=-1, keepdims=True)
            powered = jnp.exp(scores - top).astype(BF16)
            summed = jnp.where(low, value, one) if half == 0 else jnp.where(low, one, value)
            result.append((top, jnp.dot(powered, summed, preferred_element_type=F32)))
        return result

    near = chunk(0)
    res_right = remote(res.at[1], res.at[0], r_ss.at[0], r_rs.at[0], right)
    res_left = remote(res.at[1], res.at[2], r_ss.at[1], r_rs.at[1], left)
    pl.when(has_right)(res_right.start)
    pl.when(has_left)(res_left.start)
    for slot in range(9, 16):
        arrived(slot)
    far = chunk(1)

    tops = []
    sums = []
    for half in range(2):
        top_a, sum_a = near[half]
        top_b, sum_b = far[half]
        top = jnp.maximum(top_a, top_b)
        tops.append(top)
        sums.append(jnp.exp(top_a - top) * sum_a + jnp.exp(top_b - top) * sum_b)
    total = pltpu.roll(jnp.where(low, sums[1], sums[0]), HEAD, 1)
    a_send[:, :64] = (jnp.where(low, sums[0], sums[1]) / total).astype(BF16).reshape(SLAB, 64, WIDE)
    level = jnp.where(low, tops[0], tops[1]) + jnp.log(total)
    block = lax.rem(lax.broadcasted_iota(jnp.int32, (512, WIDE), 0) // ROWS, 4)
    place_of = lax.rem(lax.broadcasted_iota(jnp.int32, (512, WIDE), 1), HEAD) - 8 * block
    stats = jnp.zeros((512, WIDE), F32)
    for step in range(3):
        rounded = level.astype(BF16).astype(F32)
        stats = jnp.where(place_of == step, rounded, stats)
        level = level - rounded
    a_send[:, 64:] = jnp.sum(stats.reshape(SLAB, 4, ROWS, WIDE), axis=1).astype(BF16)

    for step in slab_steps:
        owner = lax.rem(xc + step, SLAB)
        start(remote(a_send.at[owner], a_recv.at[xc], a_ss.at[step], a_rs.at[step], at_slab(step)))
    a_recv[xc] = a_send[xc]
    row_id = lax.broadcasted_iota(jnp.int32, (WIDE, WIDE), 0)
    col_id = lax.broadcasted_iota(jnp.int32, (WIDE, WIDE), 1)
    same_half = (row_id // HEAD == col_id // HEAD) & (lax.rem(row_id, 8) < 3)
    picks = [
        jnp.where(same_half & (lax.rem(row_id, HEAD) // 8 == g), 1.0, 0.0).astype(BF16) for g in range(4)
    ]
    for step in slab_steps[::-1]:
        sender = lax.rem(xc + SLAB - step, SLAB)
        remote(a_recv.at[sender], a_recv.at[sender], a_ss.at[step], a_rs.at[step], right).wait_recv()
    packed = a_recv[:, 64:].reshape(SLAB * ROWS, WIDE)
    for g in range(4):
        levels = jnp.dot(packed, picks[g], preferred_element_type=F32).reshape(SLAB, ROWS, WIDE)
        weights = jnp.exp(levels - jnp.max(levels, axis=0, keepdims=True))
        parts = a_recv[:, ROWS * g : ROWS * (g + 1)].astype(F32)
        ctx_own[g] = (jnp.sum(weights * parts, axis=0) / jnp.sum(weights, axis=0)).astype(BF16)

    edges = []
    for slab in (1, 2, 0, 3):
        home_device = member(slab) * SLAB + xc
        for place in (0, 2, 1):
            target = home_device + 1 - place
            if place == 1:
                exists = slab != mine
                target = home_device
            else:
                exists = (target >= 0) & (target < 128)
            copy = remote(
                ctx_own.at[slab], ctx.at[mine, place], c_ss.at[slab, place], c_rs.at[mine, place],
                jnp.clip(target, 0, 127),
            )
            pl.when(exists)(copy.start)
            edges.append((exists, copy))
    ctx[mine, 1] = ctx_own[mine]
    for copy in sent:
        copy.wait_send()

    for load in loads[4:]:
        load.wait()
    def ctx_arrived(group, place):
        remote(ctx.at[group, place], ctx.at[group, place], c_ss.at[0, 0], c_rs.at[group, place], right).wait_recv()

    for turn in range(1, 4):
        ctx_arrived(lax.rem(mine + turn, 4), 1)

    def receive_edge(place):
        for group in range(4):
            ctx_arrived(group, place)

    def blank(place):
        res[place] = jnp.zeros((ROWS, 1024), BF16)
        for group in range(4):
            ctx[group, place] = jnp.zeros((ROWS, WIDE), BF16)

    pl.when(has_left)(remote(res.at[1], res.at[0], r_ss.at[0], r_rs.at[0], right).wait_recv)
    pl.when(has_right)(remote(res.at[1], res.at[2], r_ss.at[1], r_rs.at[1], left).wait_recv)
    pl.when(has_left)(lambda: receive_edge(0))
    pl.when(has_right)(lambda: receive_edge(2))
    pl.when(jnp.logical_not(has_left))(lambda: blank(0))
    pl.when(jnp.logical_not(has_right))(lambda: blank(2))

    frames = (me - 1) * ROWS + lax.broadcasted_iota(jnp.int32, (48, 1), 0)
    inside = jnp.where((frames >= 0) & (frames < limit), 1.0, 0.0)
    context = jnp.concatenate([ctx[group].reshape(48, WIDE) for group in range(4)], axis=1)
    projected = jnp.dot(context, wo[...], preferred_element_type=F32)
    mixed = res[...].reshape(48, 1024).astype(F32) + inside * projected
    average = jnp.mean(mixed, axis=-1, keepdims=True)
    centred = mixed - average
    variance = jnp.mean(centred * centred, axis=-1, keepdims=True)
    normed = (centred * lax.rsqrt(variance + 1e-05) * gain[...] + bias[...]).astype(BF16)
    lifted = jnp.dot(normed, wi[...], preferred_element_type=F32)
    gated[...] = (inside * lifted[:, :512] * jax.nn.sigmoid(lifted[:, 512:])).astype(BF16).astype(F32)
    filtered = taps[0:1, :] * gated[1 : 1 + ROWS, :]
    for tap in range(1, 31):
        filtered = filtered + taps[tap : tap + 1, :] * gated[tap + 1 : tap + 1 + ROWS, :]
    shifted = filtered * scale[...] + shift[...]
    activated = (shifted * jax.nn.sigmoid(shifted)).astype(BF16)
    out_ref[...] = (mixed[ROWS : 2 * ROWS] + jnp.dot(activated, wc[...], preferred_element_type=F32)).astype(BF16)

    pl.when(has_right)(res_right.wait_send)
    pl.when(has_left)(res_left.wait_send)
    for exists, copy in edges:
        pl.when(exists)(copy.wait_send)


def on_device(
    queries, keys, values, residual, lengths, out_proj, ln_gain, ln_bias, conv_in, taps, bn_scale, bn_shift, conv_out
):
    hbm = pl.BlockSpec(memory_space=pltpu.HBM)
    dma = pltpu.SemaphoreType.DMA

    def stay(array):
        return pltpu.with_memory_space_constraint(array, pltpu.HBM)

    def row(array):
        return stay(array.reshape(1, -1))

    return pl.pallas_call(
        kernel,
        out_shape=jax.ShapeDtypeStruct((ROWS, 1024), BF16),
        in_specs=[hbm] * 4 + [pl.BlockSpec(memory_space=pltpu.SMEM)] + [hbm] * 8,
        out_specs=pl.BlockSpec(memory_space=pltpu.VMEM),
        scratch_shapes=[
            pltpu.VMEM((ROWS, 512), BF16),
            pltpu.VMEM((ROWS, 512), BF16),
            pltpu.VMEM((ROWS, 512), BF16),
            pltpu.VMEM((3, ROWS, 1024), BF16),
            pltpu.VMEM((512, 1024), BF16),
            pltpu.VMEM((1, 1024), F32),
            pltpu.VMEM((1, 1024), F32),
            pltpu.VMEM((1024, 1024), BF16),
            pltpu.VMEM((31, 512), F32),
            pltpu.VMEM((1, 512), F32),
            pltpu.VMEM((1, 512), F32),
            pltpu.VMEM((512, 1024), BF16),
            pltpu.VMEM((4, 2, ROWS, WIDE), BF16),
            pltpu.VMEM((NZ, 2, ROWS, WIDE), BF16),
            pltpu.VMEM((4, ROWS, WIDE), BF16),
            pltpu.VMEM((SLAB, 4, ROWS, WIDE), BF16),
            pltpu.VMEM((SLAB, 80, WIDE), BF16),
            pltpu.VMEM((SLAB, 80, WIDE), BF16),
            pltpu.VMEM((4, ROWS, WIDE), BF16),
            pltpu.VMEM((4, 3, ROWS, WIDE), BF16),
            pltpu.VMEM((48, 512), F32),
            dma((12,)),
            dma((NZ,)),
            dma((NZ,)),
            dma((12,)),
            dma((12,)),
            dma((2,)),
            dma((2,)),
            dma((SLAB,)),
            dma((SLAB,)),
            dma((4, 3)),
            dma((4, 3)),
        ],
        compiler_params=pltpu.CompilerParams(
            collective_id=0, has_side_effects=True, vmem_limit_bytes=40 * 1024 * 1024
        ),
        name="conformer",
    )(
        stay(queries), stay(keys), stay(values), stay(residual), lengths, stay(out_proj), row(ln_gain), row(ln_bias),
        stay(conv_in), stay(taps), row(bn_scale), row(bn_shift), stay(conv_out),
    )


def solution(mesh):
    rows = P(("dp", "seq"), None)
    return jax.shard_map(
        on_device,
        mesh=mesh,
        in_specs=(rows, rows, rows, rows, P("dp")) + (P(),) * 8,
        out_specs=rows,
        check_vma=False,
    )
```

```python
import math

import jax
import jax.numpy as jnp
from jax import lax
from jax.experimental import pallas as pl
from jax.experimental.pallas import tpu as pltpu
from jax.sharding import PartitionSpec as P

MESH = pl.DeviceIdType.MESH
BF16 = jnp.bfloat16
F32 = jnp.float32

NZ = 16
SLAB = 8
ROWS = 16
WIDE = 128
HEAD = 64


def slot_of(offset):
    return 15 if offset in (8, -8) else 2 * abs(offset) - (1 if offset > 0 else 0)


FIRST = (4, -4, 3, -3, 2, -2, 1, -1)
RELAYS = ((-1, 4), (1, -4), (-2, 4), (2, -4), (-3, 4), (3, -4), (-4, 4))


def kernel(
    q_hbm, k_hbm, v_hbm, res_hbm, len_ref, wo_hbm, gain_hbm, bias_hbm, wi_hbm, taps_hbm, scale_hbm, shift_hbm, wc_hbm,
    out_ref,
    q_in, k_in, v_in, res, wo, gain, bias, wi, taps, scale, shift, wc,
    kv_own, kv, q_own, q_all, a_send, a_recv, ctx_own, ctx, gated,
    in_sem, kv_ss, kv_rs, q_ss, q_rs, r_ss, r_rs, a_ss, a_rs, c_ss, c_rs,
):
    me = lax.axis_index("seq")
    z = me // SLAB
    xc = lax.rem(me, SLAB)
    mine = lax.rem(z + 1, 4)
    limit = len_ref[0]

    def at_z(offset):
        return lax.rem(z + offset + NZ, NZ) * SLAB + xc

    def at_slab(step):
        return z * SLAB + lax.rem(xc + step, SLAB)

    def member(place):
        return lax.rem(z - mine + place + NZ, NZ)

    has_left = me != 0
    has_right = me != 127
    left = jnp.maximum(me - 1, 0)
    right = jnp.minimum(me + 1, 127)
    slab_steps = (4, 3, 5, 2, 6, 7, 1)

    barrier = pltpu.get_barrier_semaphore()

    def greet(target):
        pl.semaphore_signal(barrier, inc=1, device_id={"seq": target}, device_id_type=MESH)

    for d in FIRST[:6]:
        greet(at_z(d))
    for step in slab_steps:
        greet(at_slab(step))
    for d in FIRST[6:]:
        greet(at_z(d))

    loads = [
        pltpu.make_async_copy(src, dst, in_sem.at[i])
        for i, (src, dst) in enumerate(
            (
                (k_hbm, k_in), (v_hbm, v_in), (q_hbm, q_in), (res_hbm, res.at[1]),
                (wo_hbm, wo), (wi_hbm, wi), (wc_hbm, wc),
                (gain_hbm, gain), (bias_hbm, bias), (taps_hbm, taps), (scale_hbm, scale), (shift_hbm, shift),
            )
        )
    ]
    for load in loads:
        load.start()
    for load in loads[:3]:
        load.wait()
    for g in range(4):
        cols = slice(WIDE * g, WIDE * (g + 1))
        kv_own[g, 0] = k_in[:, cols]
        kv_own[g, 1] = v_in[:, cols]
        q_own[g] = q_in[:, cols]
    kv[0] = kv_own[mine]
    q_all[xc, mine] = q_own[mine]
    loads[3].wait()
    pl.semaphore_wait(barrier, 15)

    def remote(src, dst, ss, rs, target):
        return pltpu.make_async_remote_copy(
            src_ref=src, dst_ref=dst, send_sem=ss, recv_sem=rs, device_id={"seq": target}, device_id_type=MESH
        )

    def first(d):
        slot = slot_of(-d)
        return remote(
            kv_own.at[lax.rem(mine + d + 4, 4)], kv.at[slot], kv_ss.at[slot], kv_rs.at[slot], at_z(d)
        )

    def relay(source, d):
        slot = slot_of(source - d)
        return remote(kv.at[slot_of(source)], kv.at[slot], kv_ss.at[slot], kv_rs.at[slot], at_z(d))

    def arrived(slot):
        remote(kv.at[slot], kv.at[slot], kv_ss.at[slot], kv_rs.at[slot], right).wait_recv()

    sent = []

    def start(copy):
        copy.start()
        sent.append(copy)

    for turn in (2, 1, 3):
        place = lax.rem(mine + turn, 4)
        start(
            remote(
                q_own.at[place], q_all.at[xc, mine], q_ss.at[turn], q_rs.at[turn], member(place) * SLAB + xc
            )
        )
    for d in FIRST:
        start(first(d))
    for source, d in RELAYS[:4]:
        arrived(slot_of(source))
        start(relay(source, d))
    for turn in (2, 1, 3):
        place = lax.rem(mine + 4 - turn, 4)
        remote(q_own.at[0], q_all.at[xc, place], q_ss.at[turn], q_rs.at[turn], right).wait_recv()
    for step in slab_steps:
        start(remote(q_all.at[xc], q_all.at[xc], q_ss.at[4 + step], q_rs.at[4 + step], at_slab(step)))

    for source, d in RELAYS[4:]:
        arrived(slot_of(source))
        start(relay(source, d))

    for step in slab_steps:
        sender = lax.rem(xc + SLAB - step, SLAB)
        remote(q_all.at[sender], q_all.at[sender], q_ss.at[4 + step], q_rs.at[4 + step], right).wait_recv()
    arrived(slot_of(4))

    lane = lax.broadcasted_iota(jnp.int32, (1, WIDE), 1)
    low = lane < HEAD
    tile = q_all[...].reshape(512, WIDE) * jnp.asarray(1.0 / math.sqrt(HEAD), BF16)
    zero = jnp.zeros_like(tile)
    queries = (jnp.where(low, tile, zero), jnp.where(low, zero, tile))

    def chunk(part):
        slot = 8 * part + lane // ROWS
        away = (slot + 1) // 2
        offset = jnp.where(lax.rem(slot, 2) == 1, away, -away)
        source = lax.rem(z + offset + NZ, NZ)
        frame = (source * SLAB + xc) * ROWS + lax.rem(lane, ROWS)
        valid = frame < limit
        key = kv[8 * part : 8 * part + 8, 0].reshape(128, WIDE)
        value = kv[8 * part : 8 * part + 8, 1].reshape(128, WIDE)
        one = jnp.ones_like(value)
        result = []
        for half in range(2):
            scores = lax.dot_general(queries[half], key, (((1,), (1,)), ((), ())), preferred_element_type=F32)
            scores = jnp.where(valid, scores, -1e30)
            top = jnp.max(scores, axis=-1, keepdims=True)
            powered = jnp.exp(scores - top).astype(BF16)
            summed = jnp.where(low, value, one) if half == 0 else jnp.where(low, one, value)
            result.append((top, jnp.dot(powered, summed, preferred_element_type=F32)))
        return result

    near = chunk(0)
    res_right = remote(res.at[1], res.at[0], r_ss.at[0], r_rs.at[0], right)
    res_left = remote(res.at[1], res.at[2], r_ss.at[1], r_rs.at[1], left)
    pl.when(has_right)(res_right.start)
    pl.when(has_left)(res_left.start)
    for slot in range(9, 16):
        arrived(slot)
    far = chunk(1)

    tops = []
    sums = []
    for half in range(2):
        top_a, sum_a = near[half]
        top_b, sum_b = far[half]
        top = jnp.maximum(top_a, top_b)
        tops.append(top)
        sums.append(jnp.exp(top_a - top) * sum_a + jnp.exp(top_b - top) * sum_b)
    total = pltpu.roll(jnp.where(low, sums[1], sums[0]), HEAD, 1)
    a_send[:, :64] = (jnp.where(low, sums[0], sums[1]) / total).astype(BF16).reshape(SLAB, 64, WIDE)
    level = jnp.where(low, tops[0], tops[1]) + jnp.log(total)
    block = lax.rem(lax.broadcasted_iota(jnp.int32, (512, WIDE), 0) // ROWS, 4)
    place_of = lax.rem(lax.broadcasted_iota(jnp.int32, (512, WIDE), 1), HEAD) - 8 * block
    stats = jnp.zeros((512, WIDE), F32)
    for step in range(3):
        rounded = level.astype(BF16).astype(F32)
        stats = jnp.where(place_of == step, rounded, stats)
        level = level - rounded
    a_send[:, 64:] = jnp.sum(stats.reshape(SLAB, 4, ROWS, WIDE), axis=1).astype(BF16)

    for step in slab_steps:
        owner = lax.rem(xc + step, SLAB)
        start(remote(a_send.at[owner], a_recv.at[xc], a_ss.at[step], a_rs.at[step], at_slab(step)))
    a_recv[xc] = a_send[xc]
    row_id = lax.broadcasted_iota(jnp.int32, (WIDE, WIDE), 0)
    col_id = lax.broadcasted_iota(jnp.int32, (WIDE, WIDE), 1)
    same_half = (row_id // HEAD == col_id // HEAD) & (lax.rem(row_id, 8) < 3)
    picks = [
        jnp.where(same_half & (lax.rem(row_id, HEAD) // 8 == g), 1.0, 0.0).astype(BF16) for g in range(4)
    ]
    for step in slab_steps[::-1]:
        sender = lax.rem(xc + SLAB - step, SLAB)
        remote(a_recv.at[sender], a_recv.at[sender], a_ss.at[step], a_rs.at[step], right).wait_recv()
    packed = a_recv[:, 64:].reshape(SLAB * ROWS, WIDE)
    for g in range(4):
        levels = jnp.dot(packed, picks[g], preferred_element_type=F32).reshape(SLAB, ROWS, WIDE)
        weights = jnp.exp(levels - jnp.max(levels, axis=0, keepdims=True))
        parts = a_recv[:, ROWS * g : ROWS * (g + 1)].astype(F32)
        ctx_own[g] = (jnp.sum(weights * parts, axis=0) / jnp.sum(weights, axis=0)).astype(BF16)

    edges = []
    mains = []
    for turn in (2, 1, 3, 0):
        slab = lax.rem(mine + turn, 4)
        home_device = member(slab) * SLAB + xc
        for place in (0, 2, 1) if turn else (0, 2):
            target = home_device + 1 - place
            copy = remote(
                ctx_own.at[slab], ctx.at[mine, place], c_ss.at[slab, place], c_rs.at[mine, place],
                jnp.clip(target, 0, 127),
            )
            if place == 1:
                copy.start()
                mains.append(copy)
            else:
                exists = (target >= 0) & (target < 128)
                pl.when(exists)(copy.start)
                edges.append((exists, copy))
    ctx[mine, 1] = ctx_own[mine]
    for copy in sent:
        copy.wait_send()

    for load in loads[4:]:
        load.wait()
    def ctx_arrived(group, place):
        remote(ctx.at[group, place], ctx.at[group, place], c_ss.at[0, 0], c_rs.at[group, place], right).wait_recv()

    for turn in range(1, 4):
        ctx_arrived(lax.rem(mine + turn, 4), 1)

    def receive_edge(place):
        for group in range(4):
            ctx_arrived(group, place)

    def blank(place):
        res[place] = jnp.zeros((ROWS, 1024), BF16)
        for group in range(4):
            ctx[group, place] = jnp.zeros((ROWS, WIDE), BF16)

    pl.when(has_left)(remote(res.at[1], res.at[0], r_ss.at[0], r_rs.at[0], right).wait_recv)
    pl.when(has_right)(remote(res.at[1], res.at[2], r_ss.at[1], r_rs.at[1], left).wait_recv)
    pl.when(has_left)(lambda: receive_edge(0))
    pl.when(has_right)(lambda: receive_edge(2))
    pl.when(jnp.logical_not(has_left))(lambda: blank(0))
    pl.when(jnp.logical_not(has_right))(lambda: blank(2))

    frames = (me - 1) * ROWS + lax.broadcasted_iota(jnp.int32, (48, 1), 0)
    inside = jnp.where((frames >= 0) & (frames < limit), 1.0, 0.0)
    context = jnp.concatenate([ctx[group].reshape(48, WIDE) for group in range(4)], axis=1)
    projected = jnp.dot(context, wo[...], preferred_element_type=F32)
    mixed = res[...].reshape(48, 1024).astype(F32) + inside * projected
    average = jnp.mean(mixed, axis=-1, keepdims=True)
    centred = mixed - average
    variance = jnp.mean(centred * centred, axis=-1, keepdims=True)
    normed = (centred * lax.rsqrt(variance + 1e-05) * gain[...] + bias[...]).astype(BF16)
    lifted = jnp.dot(normed, wi[...], preferred_element_type=F32)
    gated[...] = (inside * lifted[:, :512] * jax.nn.sigmoid(lifted[:, 512:])).astype(BF16).astype(F32)
    filtered = taps[0:1, :] * gated[1 : 1 + ROWS, :]
    for tap in range(1, 31):
        filtered = filtered + taps[tap : tap + 1, :] * gated[tap + 1 : tap + 1 + ROWS, :]
    shifted = filtered * scale[...] + shift[...]
    activated = (shifted * jax.nn.sigmoid(shifted)).astype(BF16)
    out_ref[...] = (mixed[ROWS : 2 * ROWS] + jnp.dot(activated, wc[...], preferred_element_type=F32)).astype(BF16)

    pl.when(has_right)(res_right.wait_send)
    pl.when(has_left)(res_left.wait_send)
    for copy in mains:
        copy.wait_send()
    for exists, copy in edges:
        pl.when(exists)(copy.wait_send)


def on_device(
    queries, keys, values, residual, lengths, out_proj, ln_gain, ln_bias, conv_in, taps, bn_scale, bn_shift, conv_out
):
    hbm = pl.BlockSpec(memory_space=pltpu.HBM)
    dma = pltpu.SemaphoreType.DMA

    def stay(array):
        return pltpu.with_memory_space_constraint(array, pltpu.HBM)

    def row(array):
        return stay(array.reshape(1, -1))

    return pl.pallas_call(
        kernel,
        out_shape=jax.ShapeDtypeStruct((ROWS, 1024), BF16),
        in_specs=[hbm] * 4 + [pl.BlockSpec(memory_space=pltpu.SMEM)] + [hbm] * 8,
        out_specs=pl.BlockSpec(memory_space=pltpu.VMEM),
        scratch_shapes=[
            pltpu.VMEM((ROWS, 512), BF16),
            pltpu.VMEM((ROWS, 512), BF16),
            pltpu.VMEM((ROWS, 512), BF16),
            pltpu.VMEM((3, ROWS, 1024), BF16),
            pltpu.VMEM((512, 1024), BF16),
            pltpu.VMEM((1, 1024), F32),
            pltpu.VMEM((1, 1024), F32),
            pltpu.VMEM((1024, 1024), BF16),
            pltpu.VMEM((31, 512), F32),
            pltpu.VMEM((1, 512), F32),
            pltpu.VMEM((1, 512), F32),
            pltpu.VMEM((512, 1024), BF16),
            pltpu.VMEM((4, 2, ROWS, WIDE), BF16),
            pltpu.VMEM((NZ, 2, ROWS, WIDE), BF16),
            pltpu.VMEM((4, ROWS, WIDE), BF16),
            pltpu.VMEM((SLAB, 4, ROWS, WIDE), BF16),
            pltpu.VMEM((SLAB, 80, WIDE), BF16),
            pltpu.VMEM((SLAB, 80, WIDE), BF16),
            pltpu.VMEM((4, ROWS, WIDE), BF16),
            pltpu.VMEM((4, 3, ROWS, WIDE), BF16),
            pltpu.VMEM((48, 512), F32),
            dma((12,)),
            dma((NZ,)),
            dma((NZ,)),
            dma((12,)),
            dma((12,)),
            dma((2,)),
            dma((2,)),
            dma((SLAB,)),
            dma((SLAB,)),
            dma((4, 3)),
            dma((4, 3)),
        ],
        compiler_params=pltpu.CompilerParams(
            collective_id=0, has_side_effects=True, vmem_limit_bytes=40 * 1024 * 1024
        ),
        name="conformer",
    )(
        stay(queries), stay(keys), stay(values), stay(residual), lengths, stay(out_proj), row(ln_gain), row(ln_bias),
        stay(conv_in), stay(taps), row(bn_scale), row(bn_shift), stay(conv_out),
    )


def solution(mesh):
    rows = P(("dp", "seq"), None)
    return jax.shard_map(
        on_device,
        mesh=mesh,
        in_specs=(rows, rows, rows, rows, P("dp")) + (P(),) * 8,
        out_specs=rows,
        check_vma=False,
    )
```
